128 devices in a mesh: stream: 4 (over x), cross: 32 (over z, y, core).
Axes of the slice: x: 4, y: 4, z: 4, core: 2. Of those that a mesh axis runs over, the one named last changes fastest.
Arguments:
- forcing: float32 [16, 32, 4096], P('stream', None, 'cross'), may hold values from -6 to 6
- cotangent: float32 [16, 32, 4096], P('stream', None, 'cross'), may hold values from -6 to 6
- inverses: float32 [16, 4096, 4096], P('stream', 'cross'), as said below
- flags: int32 [16, 2048], P('stream', 'cross'), may hold values from 0 to 2
Outputs:
- response: float32 [16, 32, 4096], P('stream', None, 'cross')
- forcing_grad: float32 [16, 32, 4096], P('stream', None, 'cross')
The draws below stay inside these ranges and needn't reach their ends.
Inputs may be any that keep to these rules, and one draw needn't show every extreme that they name: `inverses`: each layer's inverse is the real form of a complex 2048 x 2048 matrix: entries (2i, 2j) and (2i+1, 2j+1) are equal, entry (2i, 2j+1) is the negative of entry (2i+1, 2j).
All inputs are finite; a program needn't handle non-finite values.
Results may differ from the reference program's by a relative error of at most 0.00015.
Values sent between devices are 32-bit elements; how exact they have to be, the bound alone decides.
A program may use at most 64 MiB of HBM per device.

```python
import jax
import jax.numpy as jnp
from jax import lax

CELLS = 2048
NV = 32
WIDTH = 4096
LAYERS = 16


def draw_inverses(key, part):
    keys = jax.random.split(jax.random.fold_in(key, 17), 4)
    spread = 0.3 / jnp.sqrt(jnp.float32(CELLS))
    shape = (LAYERS, CELLS, CELLS)
    real_part = spread * jax.random.normal(keys[0], shape, jnp.float32)
    imag_part = spread * jax.random.normal(keys[1], shape, jnp.float32)
    diag_real = jax.random.uniform(keys[2], (LAYERS, CELLS), jnp.float32, 0.7, 1.3)
    diag_imag = jax.random.uniform(keys[3], (LAYERS, CELLS), jnp.float32, -0.3, 0.3)
    identity = jnp.eye(CELLS, dtype=jnp.float32)
    real_part = real_part + diag_real[:, :, None] * identity
    imag_part = imag_part + diag_imag[:, :, None] * identity
    upper = jnp.stack([real_part, -imag_part], axis=-1)
    lower = jnp.stack([imag_part, real_part], axis=-1)
    joined = jnp.stack([upper, lower], axis=2)
    return joined.reshape(LAYERS, 2 * CELLS, 2 * CELLS).astype(jnp.float32)


def draw_flags(key, part):
    raw = jax.random.randint(jax.random.fold_in(key, 29), (LAYERS, CELLS), 0, 10)
    return jnp.where(raw < 8, 0, jnp.where(raw < 9, 1, 2)).astype(jnp.int32)


def level_of(rng, shape, pieces, low, largest):
    def one(position, blocks):
        draws = jax.random.uniform(jax.random.fold_in(jax.random.fold_in(rng, 6), position), (blocks,), jnp.float32, low / len(pieces), largest / len(pieces))
        return jnp.repeat(jnp.exp(draws), shape[position] // blocks).reshape((-1,) + (1,) * (len(shape) - position - 1))

    loudness = one(*pieces[0])
    for cut in pieces[1:]:
        loudness = loudness * one(*cut)
    return loudness


def gaussian(stream_key, extent, scale, most, shards=(), kind=jnp.bfloat16):
    entries = jax.random.normal(stream_key, extent, jnp.float32) * scale
    if len(shards) > 0:
        entries = level_of(stream_key, extent, shards, -0.22, 0.18) * entries
    return jnp.clip(entries, min=-most, max=most).astype(kind)


def setup_inputs(seed: int = 0) -> dict:
    key_list = jax.random.split(jax.random.key(seed), 5)
    return {
        "forcing": gaussian(key_list[0], (LAYERS, NV, WIDTH), 1.0, 6.0, ((0, 4), (2, 32)), jnp.float32),
        "cotangent": gaussian(key_list[1], (LAYERS, NV, WIDTH), 1.0, 6.0, ((0, 4), (2, 32)), jnp.float32),
        "inverses": draw_inverses(jax.random.fold_in(key_list[4], 71), 0),
        "flags": draw_flags(jax.random.fold_in(key_list[4], 71), 0),
    }


def penalty(flag_cells):
    factor = jnp.where(flag_cells == 0, 0.98, jnp.where(flag_cells == 1, 0.05, 0.5)).astype(jnp.float32)
    return jnp.repeat(factor, 2, axis=-1)


def reference(forcing, cotangent, inverses, flags):
    factors = penalty(flags)
    blank = jnp.zeros((NV, 2 * CELLS), jnp.float32)

    def forward_layer(previous, layer):
        matrix, drive, factor = layer
        source = drive + factor * previous
        result = jnp.dot(source, matrix.T, precision=lax.Precision.HIGHEST, preferred_element_type=jnp.float32)
        return result, result

    final_forward, response = lax.scan(forward_layer, blank, (inverses, forcing, factors))

    def backward_layer(carried, layer):
        matrix, sink, factor = layer
        source = sink + carried
        gradient = jnp.dot(source, matrix, precision=lax.Precision.HIGHEST, preferred_element_type=jnp.float32)
        return factor * gradient, gradient

    final_backward, forcing_grad = lax.scan(backward_layer, blank, (inverses, cotangent, factors), reverse=True)
    return response, forcing_grad
```

```python
import jax
import jax.numpy as jnp
from jax import lax
from jax.experimental import pallas as pl
from jax.experimental.pallas import tpu as pltpu
from jax.sharding import PartitionSpec as P

MESH = pl.DeviceIdType.MESH
SIDE = 4
CHIPS = SIDE * SIDE
HOPS = sorted(
    ((dz, dy) for dz in range(SIDE) for dy in range(SIDE)),
    key=lambda d: min(d[0], SIDE - d[0]) + min(d[1], SIDE - d[1]),
)
LAYERS = 4
HALF = 16
ROWS = 128
WIDE = 256
F32, BF16 = jnp.float32, jnp.bfloat16


def penalty(flag_cells):
    factor = jnp.where(flag_cells == 0, 0.98, jnp.where(flag_cells == 1, 0.05, 0.5)).astype(F32)
    return jnp.repeat(factor, 2, axis=-1)


def split_two(value):
    high = value.astype(BF16)
    return high, (value - high.astype(F32)).astype(BF16)


def permuted(value, table):
    high = value.astype(BF16)
    rest = value - high.astype(F32)
    mid = rest.astype(BF16)
    low = (rest - mid.astype(F32)).astype(BF16)
    return sum(jnp.dot(part, table, preferred_element_type=F32) for part in (high, mid, low))


def kernel(
    forcing, cotangent, factor, inverses, response, gradient,
    own, even, weights, planar_of, real_of, mixed,
    drive, sink, factors, got_f, put_b, got_b, carry, out_put, out_got,
    load_sem, even_put, even_sem, mixed_put, mixed_sem, side_put, side_sem,
    f_put, f_put_self, f_sem, b_put, b_sem, carry_put, carry_sem, out_put_sem, out_sem,
):
    x = lax.axis_index("stream")
    me = lax.axis_index("cross")
    sections = lax.axis_size("stream")
    core = lax.rem(me, 2)
    chip = me // 2
    zc, yc = chip // SIDE, lax.rem(chip, SIDE)
    partner = me + 1 - 2 * core

    def chip_at(k, sign):
        dz, dy = HOPS[k]
        return lax.rem(zc + sign * dz + SIDE, SIDE) * SIDE + lax.rem(yc + sign * dy + SIDE, SIDE)

    def wait(ref, sem):
        pltpu.make_async_copy(ref, ref, sem).wait()

    def remote(src, dst, send_sem, recv_sem, section, device):
        return pltpu.make_async_remote_copy(
            src_ref=src, dst_ref=dst, send_sem=send_sem, recv_sem=recv_sem,
            device_id={"stream": section, "cross": device}, device_id_type=MESH,
        )

    barrier = pltpu.get_barrier_semaphore()

    def greet(section, device):
        pl.semaphore_signal(
            barrier, inc=1, device_id={"stream": section, "cross": device}, device_id_type=MESH
        )

    greet(x, partner)

    @pl.loop(1, CHIPS)
    def _(o):
        greet(x, lax.rem(chip + o, CHIPS) * 2 + core)

    @pl.when(x > 0)
    def _():
        @pl.loop(0, CHIPS)
        def _(o):
            greet(x - 1, o * 2 + core)

    @pl.when(x < sections - 1)
    def _():
        @pl.loop(0, CHIPS)
        def _(o):
            greet(x + 1, o * 2 + core)

    first_forward = x < sections // 2

    def layer_of(forward, i):
        f = forward.astype(jnp.int32)
        return f * i + (1 - f) * (LAYERS - 1 - i)

    @pl.loop(0, LAYERS)
    def _(i):
        l = layer_of(first_forward, i)
        for j in range(2 * CHIPS):
            pltpu.make_async_copy(
                inverses.at[l, :, pl.ds(j * ROWS, ROWS)], own.at[l, j], load_sem.at[l]
            ).start()

    r = lax.broadcasted_iota(jnp.int32, (WIDE, WIDE), 0)
    k = lax.broadcasted_iota(jnp.int32, (WIDE, WIDE), 1)
    planar_of[...] = (r == 2 * (k % ROWS) + k // ROWS).astype(F32).astype(BF16)
    real_of[...] = (k == 2 * (r % ROWS) + r // ROWS).astype(F32).astype(BF16)
    mine = pl.ds(pl.multiple_of(HALF * core, HALF), HALF)
    theirs = pl.ds(pl.multiple_of(HALF * (1 - core), HALF), HALF)
    mixed[core, 0:4] = forcing[:, mine, :]
    mixed[core, 4:8] = cotangent[:, mine, :]
    mixed[core, 8:12] = factor[...]

    beside = (x > 0).astype(jnp.int32) + (x < sections - 1).astype(jnp.int32)
    pl.semaphore_wait(barrier, CHIPS + CHIPS * beside)

    mixed_copies = [
        remote(src, mixed.at[core, pl.ds(4 * j, 4)], mixed_put.at[j], mixed_sem.at[j], x, partner)
        for j, src in enumerate((forcing.at[:, theirs, :], cotangent.at[:, theirs, :], factor))
    ]
    for copy in mixed_copies:
        copy.start()

    @pl.loop(0, LAYERS)
    def _(i):
        l = layer_of(first_forward, i)
        wait(own.at[l], load_sem.at[l])
        for q in range(CHIPS):
            for h in range(2):
                even[l, core, q, :, h * ROWS : (h + 1) * ROWS] = own[
                    l, 2 * q + h, pl.ds(0, ROWS // 2, stride=2), :
                ]
        remote(even.at[l, core], even.at[l, core], even_put.at[l], even_sem.at[l], x, partner).start()

    for j in range(3):
        wait(mixed.at[0, pl.ds(4 * j, 4)], mixed_sem.at[j])
    tall = jnp.concatenate(
        [mixed[0].reshape(12 * HALF, ROWS), mixed[1].reshape(12 * HALF, ROWS)], axis=-1
    )
    tall = permuted(tall, planar_of[...]).reshape(12, HALF, WIDE)
    drive[0:4] = tall[0:4]
    sink[1:5] = tall[4:8]
    factors[0:4] = tall[8:12]

    def send_forward(step):
        for k in range(CHIPS - 1, 0, -1):
            remote(
                got_f.at[step, 0], got_f.at[lax.rem(step, LAYERS), k], f_put.at[step],
                f_sem.at[lax.rem(step, LAYERS), k], x + step // LAYERS, chip_at(k, 1) * 2 + core,
            ).start()

    @pl.when(x == 0)
    def _():
        got_f[0, 0] = drive[0]
        send_forward(0)

    @pl.when(x == sections - 1)
    def _():
        carry[LAYERS] = sink[LAYERS]

    @pl.when(x > 0)
    def _():
        remote(drive.at[0], drive.at[LAYERS], side_put.at[0], side_sem.at[0], x - 1, me).start()
        remote(factors.at[0], factors.at[LAYERS], side_put.at[1], side_sem.at[1], x - 1, me).start()

    @pl.when(x < sections - 1)
    def _():
        remote(sink.at[LAYERS], sink.at[0], side_put.at[2], side_sem.at[2], x + 1, me).start()

    def prepare(l):
        wait(even.at[l, core], even_sem.at[l])

        @pl.loop(0, CHIPS)
        def _(q):
            high, low = split_two(jnp.concatenate([even[l, 0, q], even[l, 1, q]], axis=0))
            both = jnp.concatenate([high, low], axis=0)
            weights[l, q] = jnp.dot(both, planar_of[...], preferred_element_type=F32).astype(BF16)

    middle = jnp.logical_and(x > 0, x < sections - 1).astype(jnp.int32)

    @pl.loop(0, 1 + (LAYERS - 1) * middle)
    def _(i):
        prepare(layer_of(first_forward, i))

    def prepare_next(phase, i, forward):
        @pl.when(jnp.logical_and(jnp.logical_and(phase == 0, middle == 0), i < LAYERS - 1))
        def _():
            prepare(layer_of(forward, i + 1))

    def put_out(kind, l, value, out):
        real = permuted(value, real_of[...])
        out_put[kind, l, 0] = real[:, :ROWS]
        out_put[kind, l, 1] = real[:, ROWS:]
        out[l, mine, :] = out_put[kind, l, core]
        remote(
            out_put.at[kind, l, 1 - core], out_got.at[kind, l], out_put_sem.at[kind, l],
            out_sem.at[kind, l], x, partner,
        ).start()

    def forward_step(phase, i):
        l = i

        @pl.when(jnp.logical_and(l == 0, x > 0))
        def _():
            wait(got_f.at[0, 0], f_sem.at[0, 0])

        total = jnp.zeros((4 * HALF, WIDE), F32)
        for k in range(CHIPS):
            if k > 0:
                wait(got_f.at[l, k], f_sem.at[l, k])
            high, low = split_two(got_f[l, k])
            left = jnp.concatenate([high, low], axis=0)
            turned = jnp.concatenate([left[:, ROWS:], -left[:, :ROWS]], axis=1)
            left = jnp.concatenate([left, turned], axis=0)
            total = total + lax.dot_general(
                left, weights[l, chip_at(k, -1)], (((1,), (1,)), ((), ())), preferred_element_type=F32
            )
        total = total[:, :ROWS] + total[:, ROWS:]
        result = jnp.concatenate(
            [total[:HALF] + total[HALF : 2 * HALF], total[2 * HALF : 3 * HALF] + total[3 * HALF :]], axis=1
        )

        @pl.when(jnp.logical_and(l == LAYERS - 1, x < sections - 1))
        def _():
            wait(drive.at[LAYERS], side_sem.at[0])
            wait(factors.at[LAYERS], side_sem.at[1])

        @pl.when(jnp.logical_or(l < LAYERS - 1, x < sections - 1))
        def _():
            got_f[l + 1, 0] = drive[l + 1] + factors[l + 1] * result
            send_forward(l + 1)

            @pl.when(l == LAYERS - 1)
            def _():
                remote(
                    got_f.at[LAYERS, 0], got_f.at[0, 0], f_put_self, f_sem.at[0, 0], x + 1, me
                ).start()

        put_out(0, l, result, response)
        prepare_next(phase, i, jnp.bool_(True))

    def backward_step(phase, i):
        l = LAYERS - 1 - i

        @pl.when(jnp.logical_and(l == LAYERS - 1, x < sections - 1))
        def _():
            wait(carry.at[LAYERS], carry_sem)

        high, low = split_two(carry[l + 1])
        column = jnp.concatenate(
            [high[:, :ROWS], high[:, ROWS:], low[:, :ROWS], low[:, ROWS:]], axis=0
        )
        left = jnp.concatenate([column, column], axis=1)
        for k in range(CHIPS - 1, -1, -1):
            to = chip_at(k, 1)
            part = jnp.dot(left, weights[l, to], preferred_element_type=F32)
            part = part[: 2 * HALF] + part[2 * HALF :]
            real, imag = part[:HALF], part[HALF:]
            part = jnp.concatenate(
                [real[:, :ROWS] - imag[:, ROWS:], real[:, ROWS:] + imag[:, :ROWS]], axis=1
            )
            if k > 0:
                put_b[l, k] = part
                remote(
                    put_b.at[l, k], got_b.at[l, k], b_put.at[l], b_sem.at[l, k], x, to * 2 + core
                ).start()
            else:
                got_b[l, 0] = part
        prepare_next(phase, i, jnp.bool_(False))
        total = got_b[l, 0]
        for k in range(1, CHIPS):
            wait(got_b.at[l, k], b_sem.at[l, k])
            total = total + got_b[l, k]

        @pl.when(jnp.logical_and(l == 0, x > 0))
        def _():
            wait(sink.at[0], side_sem.at[2])

        @pl.when(jnp.logical_or(l > 0, x > 0))
        def _():
            carry[l] = sink[l] + factors[l] * total

        @pl.when(jnp.logical_and(l == 0, x > 0))
        def _():
            remote(carry.at[0], carry.at[LAYERS], carry_put, carry_sem, x - 1, me).start()

        put_out(1, l, total, gradient)

    @pl.loop(0, 2)
    def _(phase):
        forward = (phase == 0) == first_forward

        @pl.when(forward)
        def _():
            @pl.loop(0, LAYERS)
            def _(i):
                forward_step(phase, i)

        @pl.when(jnp.logical_not(forward))
        def _():
            @pl.loop(0, LAYERS)
            def _(i):
                backward_step(phase, i)

    for j in range(3):
        wait(mixed.at[0, pl.ds(4 * j, 4)], mixed_put.at[j])

    @pl.loop(0, LAYERS)
    def _(l):
        wait(even.at[l, core], even_put.at[l])
        wait(put_b.at[l, pl.ds(1, CHIPS - 1)], b_put.at[l])

    @pl.when(x == 0)
    def _():
        wait(got_f.at[0, pl.ds(1, CHIPS - 1)], f_put.at[0])

    @pl.loop(1, LAYERS)
    def _(l):
        wait(got_f.at[0, pl.ds(1, CHIPS - 1)], f_put.at[l])

    @pl.when(x < sections - 1)
    def _():
        wait(got_f.at[0, pl.ds(1, CHIPS - 1)], f_put.at[LAYERS])
        wait(got_f.at[0, 0], f_put_self)
        wait(sink.at[0], side_put.at[2])

    @pl.when(x > 0)
    def _():
        wait(drive.at[0], side_put.at[0])
        wait(factors.at[0], side_put.at[1])
        wait(carry.at[0], carry_put)

    for kind, out in enumerate((response, gradient)):
        @pl.loop(0, LAYERS)
        def _(l):
            wait(out_got.at[kind, l], out_sem.at[kind, l])
            out[l, theirs, :] = out_got[kind, l]
            wait(out_got.at[kind, l], out_put_sem.at[kind, l])


def shards(forcing, cotangent, inverses, flags):
    factor = jnp.broadcast_to(penalty(flags)[:, None, :], (LAYERS, HALF, ROWS))
    vmem = pl.BlockSpec(memory_space=pltpu.VMEM)
    dma = pltpu.SemaphoreType.DMA
    block = (HALF, WIDE)
    return tuple(
        pl.pallas_call(
            kernel,
            out_shape=[jax.ShapeDtypeStruct(forcing.shape, F32)] * 2,
            in_specs=[vmem, vmem, vmem, pl.BlockSpec(memory_space=pl.ANY)],
            out_specs=[vmem, vmem],
            scratch_shapes=[
                pltpu.VMEM((LAYERS, 2 * CHIPS, ROWS, ROWS), F32),
                pltpu.VMEM((LAYERS, 2, CHIPS, ROWS // 2, WIDE), F32),
                pltpu.VMEM((LAYERS, CHIPS, WIDE, WIDE), BF16),
                pltpu.VMEM((WIDE, WIDE), BF16),
                pltpu.VMEM((WIDE, WIDE), BF16),
                pltpu.VMEM((2, 12, HALF, ROWS), F32),
                pltpu.VMEM((LAYERS + 1, *block), F32),
                pltpu.VMEM((LAYERS + 1, *block), F32),
                pltpu.VMEM((LAYERS + 1, *block), F32),
                pltpu.VMEM((LAYERS + 1, CHIPS, *block), F32),
                pltpu.VMEM((LAYERS, CHIPS, *block), F32),
                pltpu.VMEM((LAYERS, CHIPS, *block), F32),
                pltpu.VMEM((LAYERS + 1, *block), F32),
                pltpu.VMEM((2, LAYERS, 2, HALF, ROWS), F32),
                pltpu.VMEM((2, LAYERS, HALF, ROWS), F32),
                dma((LAYERS,)),
                dma((LAYERS,)),
                dma((LAYERS,)),
                dma((3,)),
                dma((3,)),
                dma((3,)),
                dma((3,)),
                dma((LAYERS + 1,)),
                dma,
                dma((LAYERS, CHIPS)),
                dma((LAYERS,)),
                dma((LAYERS, CHIPS)),
                dma,
                dma,
                dma((2, LAYERS)),
                dma((2, LAYERS)),
            ],
            compiler_params=pltpu.CompilerParams(
                collective_id=0, has_side_effects=True, vmem_limit_bytes=60 << 20
            ),
        )(forcing, cotangent, factor, inverses)
    )


def solution(mesh):
    in_specs = (
        P("stream", None, "cross"),
        P("stream", None, "cross"),
        P("stream", "cross", None),
        P("stream", "cross"),
    )
    out_specs = (P("stream", None, "cross"), P("stream", None, "cross"))
    return jax.shard_map(shards, mesh=mesh, in_specs=in_specs, out_specs=out_specs, check_vma=False)
```

```python
import jax
import jax.numpy as jnp
from jax import lax
from jax.experimental import pallas as pl
from jax.experimental.pallas import tpu as pltpu
from jax.sharding import PartitionSpec as P

MESH = pl.DeviceIdType.MESH
SIDE = 4
CHIPS = SIDE * SIDE
HOPS = sorted(
    ((dz, dy) for dz in range(SIDE) for dy in range(SIDE)),
    key=lambda d: min(d[0], SIDE - d[0]) + min(d[1], SIDE - d[1]),
)
GROUPS = ((0,), (1, 2, 3, 4), (5, 6, 7, 8, 9, 10), (11, 12, 13, 14), (15,))
PUSHES = ((15, 14, 13, 12, 11), (10, 9, 8, 7, 6, 5), (4, 3, 2, 1, 0))
LAYERS = 4
HALF = 16
ROWS = 128
WIDE = 256
F32, BF16 = jnp.float32, jnp.bfloat16


def penalty(flag_cells):
    return jnp.where(flag_cells == 0, 0.98, jnp.where(flag_cells == 1, 0.05, 0.5)).astype(F32)


def split_two(value):
    high = value.astype(BF16)
    return high, (value - high.astype(F32)).astype(BF16)


def permuted(value, table):
    high = value.astype(BF16)
    rest = value - high.astype(F32)
    mid = rest.astype(BF16)
    low = (rest - mid.astype(F32)).astype(BF16)
    return sum(jnp.dot(part, table, preferred_element_type=F32) for part in (high, mid, low))


def kernel(
    forcing, cotangent, flags, inverses, response, gradient,
    own, even, weights, planar_of, real_of, cells, factor, mixed,
    drive, sink, factors, got_f, put_b, got_b, carry, totals, back, out_put, out_got,
    load_sem, even_put, even_sem, mixed_put, mixed_sem, side_put, side_sem,
    f_put, f_put_self, f_sem, b_put, b_put_self, b_sem, back_put, back_sem, out_put_sem, out_sem,
):
    x = lax.axis_index("stream")
    me = lax.axis_index("cross")
    sections = lax.axis_size("stream")
    core = lax.rem(me, 2)
    chip = me // 2
    zc, yc = chip // SIDE, lax.rem(chip, SIDE)
    partner = me + 1 - 2 * core

    def chip_at(k, sign):
        dz, dy = HOPS[k]
        return lax.rem(zc + sign * dz + SIDE, SIDE) * SIDE + lax.rem(yc + sign * dy + SIDE, SIDE)

    def wait(ref, sem):
        pltpu.make_async_copy(ref, ref, sem).wait()

    def remote(src, dst, send_sem, recv_sem, section, device):
        return pltpu.make_async_remote_copy(
            src_ref=src, dst_ref=dst, send_sem=send_sem, recv_sem=recv_sem,
            device_id={"stream": section, "cross": device}, device_id_type=MESH,
        )

    barrier = pltpu.get_barrier_semaphore()

    def greet(section, device):
        pl.semaphore_signal(
            barrier, inc=1, device_id={"stream": section, "cross": device}, device_id_type=MESH
        )

    greet(x, partner)

    @pl.loop(1, CHIPS)
    def _(o):
        greet(x, lax.rem(chip + o, CHIPS) * 2 + core)

    @pl.when(x > 0)
    def _():
        @pl.loop(0, CHIPS)
        def _(o):
            greet(x - 1, o * 2 + core)

    @pl.when(x < sections - 1)
    def _():
        @pl.loop(0, CHIPS)
        def _(o):
            greet(x + 1, o * 2 + core)

    first_forward = x < sections // 2

    def layer_of(forward, i):
        f = forward.astype(jnp.int32)
        return f * i + (1 - f) * (LAYERS - 1 - i)

    @pl.loop(0, LAYERS)
    def _(i):
        l = layer_of(first_forward, i)
        for j in range(2 * CHIPS):
            pltpu.make_async_copy(
                inverses.at[l, :, pl.ds(j * ROWS, ROWS)], own.at[l, j], load_sem.at[l]
            ).start()

    r = lax.broadcasted_iota(jnp.int32, (WIDE, WIDE), 0)
    k = lax.broadcasted_iota(jnp.int32, (WIDE, WIDE), 1)
    planar_of[...] = (r == 2 * (k % ROWS) + k // ROWS).astype(F32).astype(BF16)
    real_of[...] = (k == 2 * (r % ROWS) + r // ROWS).astype(F32).astype(BF16)
    mine = pl.ds(pl.multiple_of(HALF * core, HALF), HALF)
    theirs = pl.ds(pl.multiple_of(HALF * (1 - core), HALF), HALF)
    cells[...] = jnp.zeros_like(cells)
    cells[0:LAYERS, 0 : ROWS // 2] = penalty(flags[...])
    twice = r[:ROWS, :ROWS] == k[:ROWS, :ROWS] // 2
    doubled = permuted(cells[...], twice.astype(F32).astype(BF16))
    for l in range(LAYERS):
        factor[l] = jnp.broadcast_to(doubled[l : l + 1], (HALF, ROWS))
    mixed[core, 0:4] = forcing[:, mine, :]
    mixed[core, 4:8] = cotangent[:, mine, :]
    mixed[core, 8:12] = factor[...]

    def extract(l):
        wait(own.at[l], load_sem.at[l])
        for q in range(CHIPS):
            for h in range(2):
                even[l, core, q, :, h * ROWS : (h + 1) * ROWS] = own[
                    l, 2 * q + h, pl.ds(0, ROWS // 2, stride=2), :
                ]

    def send_even(l):
        remote(even.at[l, core], even.at[l, core], even_put.at[l], even_sem.at[l], x, partner).start()

    extract(layer_of(first_forward, 0))
    beside = (x > 0).astype(jnp.int32) + (x < sections - 1).astype(jnp.int32)
    pl.semaphore_wait(barrier, CHIPS + CHIPS * beside)

    mixed_copies = [
        remote(src, mixed.at[core, pl.ds(4 * j, 4)], mixed_put.at[j], mixed_sem.at[j], x, partner)
        for j, src in enumerate((forcing.at[:, theirs, :], cotangent.at[:, theirs, :], factor))
    ]
    for copy in mixed_copies:
        copy.start()
    send_even(layer_of(first_forward, 0))

    def planar(j):
        wait(mixed.at[0, pl.ds(4 * j, 4)], mixed_sem.at[j])
        tall = jnp.concatenate(
            [mixed[h, 4 * j : 4 * j + 4].reshape(LAYERS * HALF, ROWS) for h in range(2)], axis=-1
        )
        return permuted(tall, planar_of[...]).reshape(LAYERS, HALF, WIDE)

    def send_forward(step):
        for k in range(CHIPS - 1, 0, -1):
            remote(
                got_f.at[step, 0], got_f.at[lax.rem(step, LAYERS), k], f_put.at[step],
                f_sem.at[lax.rem(step, LAYERS), k], x + step // LAYERS, chip_at(k, 1) * 2 + core,
            ).start()

    drive[0:LAYERS] = planar(0)

    @pl.when(x == 0)
    def _():
        got_f[0, 0] = drive[0]
        send_forward(0)

    sink[...] = planar(1)
    factors[0:LAYERS] = planar(2)

    @pl.when(x == sections - 1)
    def _():
        carry[...] = sink[LAYERS - 1]

    @pl.loop(1, LAYERS)
    def _(i):
        l = layer_of(first_forward, i)
        extract(l)
        send_even(l)

    @pl.when(x > 0)
    def _():
        remote(drive.at[0], drive.at[LAYERS], side_put.at[0], side_sem.at[0], x - 1, me).start()
        remote(factors.at[0], factors.at[LAYERS], side_put.at[1], side_sem.at[1], x - 1, me).start()

    def prepare(l):
        wait(even.at[l, core], even_sem.at[l])

        @pl.loop(0, CHIPS, unroll=4)
        def _(q):
            high, low = split_two(jnp.concatenate([even[l, 0, q], even[l, 1, q]], axis=0))
            both = jnp.concatenate([high, low], axis=0)
            weights[l, q] = jnp.dot(both, planar_of[...], preferred_element_type=F32).astype(BF16)

    middle = jnp.logical_and(x > 0, x < sections - 1).astype(jnp.int32)

    @pl.loop(0, 1 + (LAYERS - 1) * middle)
    def _(i):
        prepare(layer_of(first_forward, i))

    def prepare_next(phase, i, forward):
        @pl.when(jnp.logical_and(jnp.logical_and(phase == 0, middle == 0), i < LAYERS - 1))
        def _():
            prepare(layer_of(forward, i + 1))

    def put_out(kind, l, value, out):
        real = permuted(value, real_of[...])
        out_put[kind, l, 0] = real[:, :ROWS]
        out_put[kind, l, 1] = real[:, ROWS:]
        out[l, mine, :] = out_put[kind, l, core]
        remote(
            out_put.at[kind, l, 1 - core], out_got.at[kind, l], out_put_sem.at[kind, l],
            out_sem.at[kind, l], x, partner,
        ).start()

    def wait_side(phase, l):
        @pl.when(jnp.logical_and(jnp.logical_and(l == LAYERS - 1, x < sections - 1), phase == 0))
        def _():
            wait(drive.at[LAYERS], side_sem.at[0])
            wait(factors.at[LAYERS], side_sem.at[1])

    def forward_step(phase, i):
        l = i

        @pl.when(jnp.logical_and(l == 0, x > 0))
        def _():
            wait(got_f.at[0, 0], f_sem.at[0, 0])

        total = jnp.zeros((4 * HALF, WIDE), F32)
        for group in GROUPS:
            for k in group:
                if k > 0:
                    wait(got_f.at[l, k], f_sem.at[l, k])
            for k in group:
                high, low = split_two(got_f[l, k])
                left = jnp.concatenate([high, low], axis=0)
                turned = jnp.concatenate([left[:, ROWS:], -left[:, :ROWS]], axis=1)
                left = jnp.concatenate([left, turned], axis=0)
                total = total + lax.dot_general(
                    left, weights[l, chip_at(k, -1)], (((1,), (1,)), ((), ())), preferred_element_type=F32
                )
        total = total[:, :ROWS] + total[:, ROWS:]
        result = jnp.concatenate(
            [total[:HALF] + total[HALF : 2 * HALF], total[2 * HALF : 3 * HALF] + total[3 * HALF :]], axis=1
        )

        wait_side(phase, l)

        @pl.when(jnp.logical_or(l < LAYERS - 1, x < sections - 1))
        def _():
            got_f[l + 1, 0] = drive[l + 1] + factors[l + 1] * result
            send_forward(l + 1)

            @pl.when(l == LAYERS - 1)
            def _():
                remote(
                    got_f.at[LAYERS, 0], got_f.at[0, 0], f_put_self, f_sem.at[0, 0], x + 1, me
                ).start()

        put_out(0, l, result, response)
        prepare_next(phase, i, jnp.bool_(True))

    def summed(slot):
        total = got_b[slot, 0]
        for group in GROUPS[1:]:
            for k in group:
                wait(got_b.at[slot, k], b_sem.at[slot, k])
            for k in group:
                total = total + got_b[slot, k]
        return total

    def backward_step(phase, i):
        l = LAYERS - 1 - i

        last = l == LAYERS - 1
        inner = l < LAYERS - 1
        wait_side(phase, l)

        @pl.when(jnp.logical_or(inner, x < sections - 1))
        def _():
            @pl.when(last)
            def _():
                wait(got_b.at[LAYERS, 0], b_sem.at[LAYERS, 0])

            total = summed(l + 1)
            totals[l + 1] = total
            carry[...] = sink[l] + factors[l + 1] * total

        high, low = split_two(carry[...])
        column = jnp.concatenate(
            [high[:, :ROWS], high[:, ROWS:], low[:, :ROWS], low[:, ROWS:]], axis=0
        )
        left = jnp.concatenate([column, column], axis=1)
        leaves = jnp.logical_and(l == 0, x > 0).astype(jnp.int32)
        slot = l + LAYERS * leaves
        for group in PUSHES:
            for k in group:
                part = jnp.dot(left, weights[l, chip_at(k, 1)], preferred_element_type=F32)
                part = part[: 2 * HALF] + part[2 * HALF :]
                real, imag = part[:HALF], part[HALF:]
                put_b[l, k] = jnp.concatenate(
                    [real[:, :ROWS] - imag[:, ROWS:], real[:, ROWS:] + imag[:, :ROWS]], axis=1
                )
            for k in group:
                if k > 0:
                    remote(
                        put_b.at[l, k], got_b.at[slot, k], b_put.at[l], b_sem.at[slot, k],
                        x - leaves, chip_at(k, 1) * 2 + core,
                    ).start()

        @pl.when(leaves > 0)
        def _():
            remote(
                put_b.at[l, 0], got_b.at[LAYERS, 0], b_put_self, b_sem.at[LAYERS, 0], x - 1, me
            ).start()

        @pl.when(leaves == 0)
        def _():
            got_b[l, 0] = put_b[l, 0]

        prepare_next(phase, i, jnp.bool_(False))

        @pl.when(inner)
        def _():
            put_out(1, l + 1, totals[l + 1], gradient)

        @pl.when(jnp.logical_and(last, x < sections - 1))
        def _():
            remote(totals.at[LAYERS], back, back_put, back_sem, x + 1, me).start()

    @pl.loop(0, 2)
    def _(phase):
        forward = (phase == 0) == first_forward

        @pl.when(forward)
        def _():
            @pl.loop(0, LAYERS)
            def _(i):
                forward_step(phase, i)

        @pl.when(jnp.logical_not(forward))
        def _():
            @pl.loop(0, LAYERS)
            def _(i):
                backward_step(phase, i)

    @pl.when(x == 0)
    def _():
        back[...] = summed(0)

    @pl.when(x > 0)
    def _():
        wait(back, back_sem)

    put_out(1, 0, back[...], gradient)
    for j in range(3):
        wait(mixed.at[0, pl.ds(4 * j, 4)], mixed_put.at[j])

    @pl.loop(0, LAYERS)
    def _(l):
        wait(even.at[l, core], even_put.at[l])
        wait(put_b.at[l, pl.ds(1, CHIPS - 1)], b_put.at[l])

    @pl.when(x == 0)
    def _():
        wait(got_f.at[0, pl.ds(1, CHIPS - 1)], f_put.at[0])

    @pl.loop(1, LAYERS)
    def _(l):
        wait(got_f.at[0, pl.ds(1, CHIPS - 1)], f_put.at[l])

    @pl.when(x < sections - 1)
    def _():
        wait(got_f.at[0, pl.ds(1, CHIPS - 1)], f_put.at[LAYERS])
        wait(got_f.at[0, 0], f_put_self)
        wait(back, back_put)

    @pl.when(x > 0)
    def _():
        wait(drive.at[0], side_put.at[0])
        wait(factors.at[0], side_put.at[1])
        wait(carry, b_put_self)

    for kind, out in enumerate((response, gradient)):
        @pl.loop(0, LAYERS)
        def _(l):
            wait(out_got.at[kind, l], out_sem.at[kind, l])
            out[l, theirs, :] = out_got[kind, l]
            wait(out_got.at[kind, l], out_put_sem.at[kind, l])


def shards(forcing, cotangent, inverses, flags):
    vmem = pl.BlockSpec(memory_space=pltpu.VMEM)
    dma = pltpu.SemaphoreType.DMA
    block = (HALF, WIDE)
    return tuple(
        pl.pallas_call(
            kernel,
            out_shape=[jax.ShapeDtypeStruct(forcing.shape, F32)] * 2,
            in_specs=[vmem, vmem, vmem, pl.BlockSpec(memory_space=pl.ANY)],
            out_specs=[vmem, vmem],
            scratch_shapes=[
                pltpu.VMEM((LAYERS, 2 * CHIPS, ROWS, ROWS), F32),
                pltpu.VMEM((LAYERS, 2, CHIPS, ROWS // 2, WIDE), F32),
                pltpu.VMEM((LAYERS, CHIPS, WIDE, WIDE), BF16),
                pltpu.VMEM((WIDE, WIDE), BF16),
                pltpu.VMEM((WIDE, WIDE), BF16),
                pltpu.VMEM((8, ROWS), F32),
                pltpu.VMEM((LAYERS, HALF, ROWS), F32),
                pltpu.VMEM((2, 12, HALF, ROWS), F32),
                pltpu.VMEM((LAYERS + 1, *block), F32),
                pltpu.VMEM((LAYERS, *block), F32),
                pltpu.VMEM((LAYERS + 1, *block), F32),
                pltpu.VMEM((LAYERS + 1, CHIPS, *block), F32),
                pltpu.VMEM((LAYERS, CHIPS, *block), F32),
                pltpu.VMEM((LAYERS + 1, CHIPS, *block), F32),
                pltpu.VMEM(block, F32),
                pltpu.VMEM((LAYERS + 1, *block), F32),
                pltpu.VMEM(block, F32),
                pltpu.VMEM((2, LAYERS, 2, HALF, ROWS), F32),
                pltpu.VMEM((2, LAYERS, HALF, ROWS), F32),
                dma((LAYERS,)),
                dma((LAYERS,)),
                dma((LAYERS,)),
                dma((3,)),
                dma((3,)),
                dma((2,)),
                dma((2,)),
                dma((LAYERS + 1,)),
                dma,
                dma((LAYERS, CHIPS)),
                dma((LAYERS,)),
                dma,
                dma((LAYERS + 1, CHIPS)),
                dma,
                dma,
                dma((2, LAYERS)),
                dma((2, LAYERS)),
            ],
            compiler_params=pltpu.CompilerParams(
                collective_id=0, has_side_effects=True, vmem_limit_bytes=60 << 20
            ),
        )(forcing, cotangent, flags, inverses)
    )


def solution(mesh):
    in_specs = (
        P("stream", None, "cross"),
        P("stream", None, "cross"),
        P("stream", "cross", None),
        P("stream", "cross"),
    )
    out_specs = (P("stream", None, "cross"), P("stream", None, "cross"))
    return jax.shard_map(shards, mesh=mesh, in_specs=in_specs, out_specs=out_specs, check_vma=False)
```

```python
import jax
import jax.numpy as jnp
from jax import lax
from jax.experimental import pallas as pl
from jax.experimental.pallas import tpu as pltpu
from jax.sharding import PartitionSpec as P

MESH = pl.DeviceIdType.MESH
SIDE = 4
CHIPS = SIDE * SIDE
HOPS = sorted(
    ((dz, dy) for dz in range(SIDE) for dy in range(SIDE)),
    key=lambda d: min(d[0], SIDE - d[0]) + min(d[1], SIDE - d[1]),
)
GROUPS = ((0,), (1, 2, 3, 4), (5, 6, 7, 8, 9, 10), (11, 12, 13, 14), (15,))
PUSHES = ((15, 14, 13, 12, 11), (10, 9, 8, 7, 6, 5), (4, 3, 2, 1, 0))
LAYERS = 4
HALF = 16
SETS = 2
PART = HALF // SETS
ROWS = 128
WIDE = 256
F32, BF16 = jnp.float32, jnp.bfloat16


def penalty(flag_cells):
    return jnp.where(flag_cells == 0, 0.98, jnp.where(flag_cells == 1, 0.05, 0.5)).astype(F32)


def split_two(value):
    high = value.astype(BF16)
    return high, (value - high.astype(F32)).astype(BF16)


def permuted(value, table):
    high = value.astype(BF16)
    rest = value - high.astype(F32)
    mid = rest.astype(BF16)
    low = (rest - mid.astype(F32)).astype(BF16)
    return sum(jnp.dot(part, table, preferred_element_type=F32) for part in (high, mid, low))


def kernel(
    forcing_in, cotangent_in, flags_in, inverses, response, gradient,
    forcing, cotangent, flags, in_sem,
    own, even, weights, planar_of, real_of, cells, factor, mixed,
    drive, sink, factors, got_f, put_b, got_b, carry, totals, back, out_put, out_got,
    load_sem, even_put, even_sem, mixed_put, mixed_sem, side_put, side_sem,
    f_put, f_put_self, f_sem, b_put, b_put_self, b_sem, back_put, back_sem, out_put_sem, out_sem,
):
    x = lax.axis_index("stream")
    me = lax.axis_index("cross")
    sections = lax.axis_size("stream")
    core = lax.rem(me, 2)
    chip = me // 2
    zc, yc = chip // SIDE, lax.rem(chip, SIDE)
    partner = me + 1 - 2 * core

    def chip_at(k, sign):
        dz, dy = HOPS[k]
        return lax.rem(zc + sign * dz + SIDE, SIDE) * SIDE + lax.rem(yc + sign * dy + SIDE, SIDE)

    def wait(ref, sem):
        pltpu.make_async_copy(ref, ref, sem).wait()

    def remote(src, dst, send_sem, recv_sem, section, device):
        return pltpu.make_async_remote_copy(
            src_ref=src, dst_ref=dst, send_sem=send_sem, recv_sem=recv_sem,
            device_id={"stream": section, "cross": device}, device_id_type=MESH,
        )

    barrier = pltpu.get_barrier_semaphore()

    def greet(section, device):
        pl.semaphore_signal(
            barrier, inc=1, device_id={"stream": section, "cross": device}, device_id_type=MESH
        )

    greet(x, partner)

    @pl.loop(1, CHIPS)
    def _(o):
        greet(x, lax.rem(chip + o, CHIPS) * 2 + core)

    @pl.when(x > 0)
    def _():
        @pl.loop(0, CHIPS)
        def _(o):
            greet(x - 1, o * 2 + core)

    @pl.when(x < sections - 1)
    def _():
        @pl.loop(0, CHIPS)
        def _(o):
            greet(x + 1, o * 2 + core)

    first_forward = x < sections // 2
    inputs = ((forcing_in, forcing), (cotangent_in, cotangent), (flags_in, flags))
    for j, (src, dst) in enumerate(inputs):
        pltpu.make_async_copy(src, dst, in_sem.at[j]).start()

    def layer_of(forward, i):
        f = forward.astype(jnp.int32)
        return f * i + (1 - f) * (LAYERS - 1 - i)

    @pl.loop(0, LAYERS)
    def _(i):
        l = layer_of(first_forward, i)
        for j in range(2 * CHIPS):
            pltpu.make_async_copy(
                inverses.at[l, :, pl.ds(j * ROWS, ROWS)], own.at[l, j], load_sem.at[l]
            ).start()

    r = lax.broadcasted_iota(jnp.int32, (WIDE, WIDE), 0)
    k = lax.broadcasted_iota(jnp.int32, (WIDE, WIDE), 1)
    planar_of[...] = (r == 2 * (k % ROWS) + k // ROWS).astype(F32).astype(BF16)
    real_of[...] = (k == 2 * (r % ROWS) + r // ROWS).astype(F32).astype(BF16)
    mine = pl.ds(pl.multiple_of(HALF * core, HALF), HALF)
    theirs = pl.ds(pl.multiple_of(HALF * (1 - core), HALF), HALF)
    for j, (src, dst) in enumerate(inputs):
        pltpu.make_async_copy(src, dst, in_sem.at[j]).wait()
    cells[...] = jnp.zeros_like(cells)
    cells[0:LAYERS, 0 : ROWS // 2] = penalty(flags[...])
    twice = r[:ROWS, :ROWS] == k[:ROWS, :ROWS] // 2
    doubled = permuted(cells[...], twice.astype(F32).astype(BF16))
    for l in range(LAYERS):
        factor[l] = jnp.broadcast_to(doubled[l : l + 1], (HALF, ROWS))
    mixed[core, 0:4] = forcing[:, mine, :]
    mixed[core, 4:8] = cotangent[:, mine, :]
    mixed[core, 8:12] = factor[...]

    def extract(l):
        wait(own.at[l], load_sem.at[l])
        for q in range(CHIPS):
            for h in range(2):
                even[l, core, q, :, h * ROWS : (h + 1) * ROWS] = own[
                    l, 2 * q + h, pl.ds(0, ROWS // 2, stride=2), :
                ]

    def send_even(l):
        remote(even.at[l, core], even.at[l, core], even_put.at[l], even_sem.at[l], x, partner).start()

    extract(layer_of(first_forward, 0))
    beside = (x > 0).astype(jnp.int32) + (x < sections - 1).astype(jnp.int32)
    pl.semaphore_wait(barrier, CHIPS + CHIPS * beside)

    mixed_copies = [
        remote(src, mixed.at[core, pl.ds(4 * j, 4)], mixed_put.at[j], mixed_sem.at[j], x, partner)
        for j, src in enumerate((forcing.at[:, theirs, :], cotangent.at[:, theirs, :], factor))
    ]
    for copy in mixed_copies:
        copy.start()
    send_even(layer_of(first_forward, 0))

    def planar(j):
        wait(mixed.at[0, pl.ds(4 * j, 4)], mixed_sem.at[j])
        tall = jnp.concatenate(
            [mixed[h, 4 * j : 4 * j + 4].reshape(LAYERS * HALF, ROWS) for h in range(2)], axis=-1
        )
        return permuted(tall, planar_of[...]).reshape(LAYERS, HALF, WIDE)

    def rows_of(g):
        return slice(g * PART, (g + 1) * PART)

    def send_forward(step, g):
        slot = lax.rem(step, LAYERS)
        for k in range(CHIPS - 1, 0, -1):
            remote(
                got_f.at[step, g, 0], got_f.at[slot, g, k], f_put.at[step, g],
                f_sem.at[slot, g, k], x + step // LAYERS, chip_at(k, 1) * 2 + core,
            ).start()

    drive[0:LAYERS] = planar(0)

    @pl.when(x == 0)
    def _():
        for g in range(SETS):
            got_f[0, g, 0] = drive[0, rows_of(g)]
            send_forward(0, g)

    sink[...] = planar(1)
    factors[0:LAYERS] = planar(2)

    @pl.when(x == sections - 1)
    def _():
        carry[...] = sink[LAYERS - 1]

    @pl.loop(1, LAYERS)
    def _(i):
        l = layer_of(first_forward, i)
        extract(l)
        send_even(l)

    @pl.when(x > 0)
    def _():
        remote(drive.at[0], drive.at[LAYERS], side_put.at[0], side_sem.at[0], x - 1, me).start()
        remote(factors.at[0], factors.at[LAYERS], side_put.at[1], side_sem.at[1], x - 1, me).start()

    def prepare(l):
        wait(even.at[l, core], even_sem.at[l])

        @pl.loop(0, CHIPS, unroll=4)
        def _(q):
            high, low = split_two(jnp.concatenate([even[l, 0, q], even[l, 1, q]], axis=0))
            both = jnp.concatenate([high, low], axis=0)
            weights[l, q] = jnp.dot(both, planar_of[...], preferred_element_type=F32).astype(BF16)

    middle = jnp.logical_and(x > 0, x < sections - 1).astype(jnp.int32)

    @pl.loop(0, 1 + (LAYERS - 1) * middle)
    def _(i):
        prepare(layer_of(first_forward, i))

    def prepare_next(phase, i, forward):
        @pl.when(jnp.logical_and(jnp.logical_and(phase == 0, middle == 0), i < LAYERS - 1))
        def _():
            prepare(layer_of(forward, i + 1))

    def put_out(kind, l, value, out):
        real = permuted(value, real_of[...])
        out_put[kind, l, 0] = real[:, :ROWS]
        out_put[kind, l, 1] = real[:, ROWS:]
        out[l, mine, :] = out_put[kind, l, core]
        remote(
            out_put.at[kind, l, 1 - core], out_got.at[kind, l], out_put_sem.at[kind, l],
            out_sem.at[kind, l], x, partner,
        ).start()

    def wait_side(phase, l):
        @pl.when(jnp.logical_and(jnp.logical_and(l == LAYERS - 1, x < sections - 1), phase == 0))
        def _():
            wait(drive.at[LAYERS], side_sem.at[0])
            wait(factors.at[LAYERS], side_sem.at[1])

    def forward_set(l, g):
        @pl.when(jnp.logical_and(l == 0, x > 0))
        def _():
            wait(got_f.at[0, g, 0], f_sem.at[0, g, 0])

        total = jnp.zeros((4 * PART, WIDE), F32)
        for group in GROUPS:
            for k in group:
                if k > 0:
                    wait(got_f.at[l, g, k], f_sem.at[l, g, k])
            for k in group:
                value = got_f[l, g, k]
                turned = jnp.concatenate([value[:, ROWS:], -value[:, :ROWS]], axis=1)
                left = jnp.concatenate(split_two(jnp.concatenate([value, turned], axis=0)), axis=0)
                total = total + lax.dot_general(
                    left, weights[l, chip_at(k, -1)], (((1,), (1,)), ((), ())), preferred_element_type=F32
                )
        total = total[: 2 * PART] + total[2 * PART :]
        total = total[:, :ROWS] + total[:, ROWS:]
        result = jnp.concatenate([total[:PART], total[PART:]], axis=1)

        @pl.when(jnp.logical_or(l < LAYERS - 1, x < sections - 1))
        def _():
            got_f[l + 1, g, 0] = drive[l + 1, rows_of(g)] + factors[l + 1, rows_of(g)] * result
            send_forward(l + 1, g)

            @pl.when(l == LAYERS - 1)
            def _():
                remote(
                    got_f.at[LAYERS, g, 0], got_f.at[0, g, 0], f_put_self.at[g], f_sem.at[0, g, 0],
                    x + 1, me,
                ).start()

        return result

    def forward_step(phase, i):
        l = i
        wait_side(phase, l)
        result = jnp.concatenate([forward_set(l, g) for g in range(SETS)], axis=0)
        put_out(0, l, result, response)
        prepare_next(phase, i, jnp.bool_(True))

    def summed(slot, g):
        total = got_b[slot, g, 0]
        for group in GROUPS[1:]:
            for k in group:
                wait(got_b.at[slot, g, k], b_sem.at[slot, g, k])
            for k in group:
                total = total + got_b[slot, g, k]
        return total

    def backward_set(l, g):
        @pl.when(jnp.logical_or(l < LAYERS - 1, x < sections - 1))
        def _():
            @pl.when(l == LAYERS - 1)
            def _():
                wait(got_b.at[LAYERS, g, 0], b_sem.at[LAYERS, g, 0])

            total = summed(l + 1, g)
            totals[l + 1, rows_of(g)] = total
            carry[rows_of(g)] = sink[l, rows_of(g)] + factors[l + 1, rows_of(g)] * total

        value = carry[rows_of(g)]
        column = jnp.concatenate(
            split_two(jnp.concatenate([value[:, :ROWS], value[:, ROWS:]], axis=0)), axis=0
        )
        left = jnp.concatenate([column, column], axis=1)
        leaves = jnp.logical_and(l == 0, x > 0).astype(jnp.int32)
        slot = l + LAYERS * leaves
        for group in PUSHES:
            for k in group:
                part = jnp.dot(left, weights[l, chip_at(k, 1)], preferred_element_type=F32)
                part = part[: 2 * PART] + part[2 * PART :]
                real, imag = part[:PART], part[PART:]
                put_b[l, g, k] = jnp.concatenate(
                    [real[:, :ROWS] - imag[:, ROWS:], real[:, ROWS:] + imag[:, :ROWS]], axis=1
                )
            for k in group:
                if k > 0:
                    remote(
                        put_b.at[l, g, k], got_b.at[slot, g, k], b_put.at[l, g], b_sem.at[slot, g, k],
                        x - leaves, chip_at(k, 1) * 2 + core,
                    ).start()

        @pl.when(leaves > 0)
        def _():
            remote(
                put_b.at[l, g, 0], got_b.at[LAYERS, g, 0], b_put_self.at[g], b_sem.at[LAYERS, g, 0],
                x - 1, me,
            ).start()

        @pl.when(leaves == 0)
        def _():
            got_b[l, g, 0] = put_b[l, g, 0]

    def backward_step(phase, i):
        l = LAYERS - 1 - i
        wait_side(phase, l)
        for g in range(SETS):
            backward_set(l, g)

        @pl.when(l < LAYERS - 1)
        def _():
            put_out(1, l + 1, totals[l + 1], gradient)

        @pl.when(jnp.logical_and(l == LAYERS - 1, x < sections - 1))
        def _():
            remote(totals.at[LAYERS], back, back_put, back_sem, x + 1, me).start()

        prepare_next(phase, i, jnp.bool_(False))

    @pl.loop(0, 2)
    def _(phase):
        forward = (phase == 0) == first_forward

        @pl.when(forward)
        def _():
            @pl.loop(0, LAYERS)
            def _(i):
                forward_step(phase, i)

        @pl.when(jnp.logical_not(forward))
        def _():
            @pl.loop(0, LAYERS)
            def _(i):
                backward_step(phase, i)

    @pl.when(x == 0)
    def _():
        for g in range(SETS):
            back[rows_of(g)] = summed(0, g)

    @pl.when(x > 0)
    def _():
        wait(back, back_sem)

    put_out(1, 0, back[...], gradient)
    for j in range(3):
        wait(mixed.at[0, pl.ds(4 * j, 4)], mixed_put.at[j])

    @pl.loop(0, LAYERS)
    def _(l):
        wait(even.at[l, core], even_put.at[l])
        for g in range(SETS):
            wait(put_b.at[l, g, pl.ds(1, CHIPS - 1)], b_put.at[l, g])

    for g in range(SETS):
        sent = got_f.at[0, g, pl.ds(1, CHIPS - 1)]

        @pl.when(x == 0)
        def _():
            wait(sent, f_put.at[0, g])

        @pl.loop(1, LAYERS)
        def _(l):
            wait(sent, f_put.at[l, g])

        @pl.when(x < sections - 1)
        def _():
            wait(sent, f_put.at[LAYERS, g])
            wait(got_f.at[0, g, 0], f_put_self.at[g])

        @pl.when(x > 0)
        def _():
            wait(got_b.at[0, g, 0], b_put_self.at[g])

    @pl.when(x < sections - 1)
    def _():
        wait(back, back_put)

    @pl.when(x > 0)
    def _():
        wait(drive.at[0], side_put.at[0])
        wait(factors.at[0], side_put.at[1])

    for kind, out in enumerate((response, gradient)):
        @pl.loop(0, LAYERS)
        def _(l):
            wait(out_got.at[kind, l], out_sem.at[kind, l])
            out[l, theirs, :] = out_got[kind, l]
            wait(out_got.at[kind, l], out_put_sem.at[kind, l])


def shards(forcing, cotangent, inverses, flags):
    vmem = pl.BlockSpec(memory_space=pltpu.VMEM)
    dma = pltpu.SemaphoreType.DMA
    block = (HALF, WIDE)
    return tuple(
        pl.pallas_call(
            kernel,
            out_shape=[jax.ShapeDtypeStruct(forcing.shape, F32)] * 2,
            in_specs=[pl.BlockSpec(memory_space=pl.ANY)] * 4,
            out_specs=[vmem, vmem],
            scratch_shapes=[
                pltpu.VMEM((LAYERS, 2 * HALF, ROWS), F32),
                pltpu.VMEM((LAYERS, 2 * HALF, ROWS), F32),
                pltpu.VMEM((LAYERS, ROWS // 2), jnp.int32),
                dma((3,)),
                pltpu.VMEM((LAYERS, 2 * CHIPS, ROWS, ROWS), F32),
                pltpu.VMEM((LAYERS, 2, CHIPS, ROWS // 2, WIDE), F32),
                pltpu.VMEM((LAYERS, CHIPS, WIDE, WIDE), BF16),
                pltpu.VMEM((WIDE, WIDE), BF16),
                pltpu.VMEM((WIDE, WIDE), BF16),
                pltpu.VMEM((8, ROWS), F32),
                pltpu.VMEM((LAYERS, HALF, ROWS), F32),
                pltpu.VMEM((2, 12, HALF, ROWS), F32),
                pltpu.VMEM((LAYERS + 1, *block), F32),
                pltpu.VMEM((LAYERS, *block), F32),
                pltpu.VMEM((LAYERS + 1, *block), F32),
                pltpu.VMEM((LAYERS + 1, SETS, CHIPS, PART, WIDE), F32),
                pltpu.VMEM((LAYERS, SETS, CHIPS, PART, WIDE), F32),
                pltpu.VMEM((LAYERS + 1, SETS, CHIPS, PART, WIDE), F32),
                pltpu.VMEM(block, F32),
                pltpu.VMEM((LAYERS + 1, *block), F32),
                pltpu.VMEM(block, F32),
                pltpu.VMEM((2, LAYERS, 2, HALF, ROWS), F32),
                pltpu.VMEM((2, LAYERS, HALF, ROWS), F32),
                dma((LAYERS,)),
                dma((LAYERS,)),
                dma((LAYERS,)),
                dma((3,)),
                dma((3,)),
                dma((2,)),
                dma((2,)),
                dma((LAYERS + 1, SETS)),
                dma((SETS,)),
                dma((LAYERS, SETS, CHIPS)),
                dma((LAYERS, SETS)),
                dma((SETS,)),
                dma((LAYERS + 1, SETS, CHIPS)),
                dma,
                dma,
                dma((2, LAYERS)),
                dma((2, LAYERS)),
            ],
            compiler_params=pltpu.CompilerParams(
                collective_id=0, has_side_effects=True, vmem_limit_bytes=57 << 20
            ),
        )(forcing, cotangent, flags, inverses)
    )


def solution(mesh):
    in_specs = (
        P("stream", None, "cross"),
        P("stream", None, "cross"),
        P("stream", "cross", None),
        P("stream", "cross"),
    )
    out_specs = (P("stream", None, "cross"), P("stream", None, "cross"))
    return jax.shard_map(shards, mesh=mesh, in_specs=in_specs, out_specs=out_specs, check_vma=False)
```

```python
import jax
import jax.numpy as jnp
from jax import lax
from jax.experimental import pallas as pl
from jax.experimental.pallas import tpu as pltpu
from jax.sharding import PartitionSpec as P

MESH = pl.DeviceIdType.MESH
SIDE = 4
CHIPS = SIDE * SIDE
HOPS = sorted(
    ((dz, dy) for dz in range(SIDE) for dy in range(SIDE)),
    key=lambda d: min(d[0], SIDE - d[0]) + min(d[1], SIDE - d[1]),
)
GROUPS = ((0,), (1, 2, 3, 4), (5, 6, 7, 8, 9, 10), (11, 12, 13, 14), (15,))
PUSHES = ((15, 14, 13, 12, 11), (4, 3, 2, 1, 0), (10, 9, 8, 7, 6, 5))
LAYERS = 4
PIECES = CHIPS // SIDE
HALF = 16
SETS = 2
PART = HALF // SETS
ROWS = 128
WIDE = 256
F32, BF16 = jnp.float32, jnp.bfloat16


def penalty(flag_cells):
    return jnp.where(flag_cells == 0, 0.98, jnp.where(flag_cells == 1, 0.05, 0.5)).astype(F32)


def split_two(value):
    high = value.astype(BF16)
    return high, (value - high.astype(F32)).astype(BF16)


def permuted(value, table):
    high = value.astype(BF16)
    rest = value - high.astype(F32)
    mid = rest.astype(BF16)
    low = (rest - mid.astype(F32)).astype(BF16)
    return sum(jnp.dot(part, table, preferred_element_type=F32) for part in (high, mid, low))


def kernel(
    forcing_in, cotangent_in, flags_in, inverses, response, gradient,
    forcing, cotangent, flags, in_sem,
    own, even, weights, planar_of, real_of, cells, factor, mixed,
    drive, sink, factors, got_f, put_b, got_b, carry, totals, back, out_put, out_got,
    load_sem, even_put, even_sem, mixed_put, mixed_sem, side_put, side_sem,
    next_ready, last_ready, f_put, f_put_self, f_sem, b_put, b_put_self, b_sem, back_put, back_sem, out_put_sem, out_sem,
):
    x = lax.axis_index("stream")
    me = lax.axis_index("cross")
    sections = lax.axis_size("stream")
    core = lax.rem(me, 2)
    chip = me // 2
    zc, yc = chip // SIDE, lax.rem(chip, SIDE)
    partner = me + 1 - 2 * core

    def chip_at(k, sign):
        dz, dy = HOPS[k]
        return lax.rem(zc + sign * dz + SIDE, SIDE) * SIDE + lax.rem(yc + sign * dy + SIDE, SIDE)

    def wait(ref, sem):
        pltpu.make_async_copy(ref, ref, sem).wait()

    def remote(src, dst, send_sem, recv_sem, section, device):
        return pltpu.make_async_remote_copy(
            src_ref=src, dst_ref=dst, send_sem=send_sem, recv_sem=recv_sem,
            device_id={"stream": section, "cross": device}, device_id_type=MESH,
        )

    barrier = pltpu.get_barrier_semaphore()

    def greet(section, device):
        pl.semaphore_signal(
            barrier, inc=1, device_id={"stream": section, "cross": device}, device_id_type=MESH
        )

    greet(x, partner)

    @pl.loop(1, CHIPS)
    def _(o):
        greet(x, lax.rem(chip + o, CHIPS) * 2 + core)

    @pl.when(x > 0)
    def _():
        greet(x - 1, me)

    @pl.when(x < sections - 1)
    def _():
        greet(x + 1, me)

    first_forward = x < sections // 2
    inputs = ((forcing_in, forcing), (cotangent_in, cotangent), (flags_in, flags))
    for j, (src, dst) in enumerate(inputs):
        pltpu.make_async_copy(src, dst, in_sem.at[j]).start()

    def layer_of(forward, i):
        f = forward.astype(jnp.int32)
        return f * i + (1 - f) * (LAYERS - 1 - i)

    @pl.loop(0, LAYERS)
    def _(i):
        l = layer_of(first_forward, i)
        for j in range(2 * CHIPS):
            pltpu.make_async_copy(
                inverses.at[l, :, pl.ds(j * ROWS, ROWS)], own.at[l, j], load_sem.at[l]
            ).start()

    r = lax.broadcasted_iota(jnp.int32, (WIDE, WIDE), 0)
    k = lax.broadcasted_iota(jnp.int32, (WIDE, WIDE), 1)
    planar_of[...] = (r == 2 * (k % ROWS) + k // ROWS).astype(F32).astype(BF16)
    real_of[...] = (k == 2 * (r % ROWS) + r // ROWS).astype(F32).astype(BF16)
    mine = pl.ds(pl.multiple_of(HALF * core, HALF), HALF)
    theirs = pl.ds(pl.multiple_of(HALF * (1 - core), HALF), HALF)
    for j, (src, dst) in enumerate(inputs):
        pltpu.make_async_copy(src, dst, in_sem.at[j]).wait()
    cells[...] = jnp.zeros_like(cells)
    cells[0:LAYERS, 0 : ROWS // 2] = penalty(flags[...])
    twice = r[:ROWS, :ROWS] == k[:ROWS, :ROWS] // 2
    doubled = permuted(cells[...], twice.astype(F32).astype(BF16))
    for l in range(LAYERS):
        factor[l] = jnp.broadcast_to(doubled[l : l + 1], (HALF, ROWS))
    mixed[core, 0:4] = forcing[:, mine, :]
    mixed[core, 4:8] = cotangent[:, mine, :]
    mixed[core, 8:12] = factor[...]

    def extract(l):
        wait(own.at[l], load_sem.at[l])
        for q in range(CHIPS):
            for h in range(2):
                even[l, core, q, :, h * ROWS : (h + 1) * ROWS] = own[
                    l, 2 * q + h, pl.ds(0, ROWS // 2, stride=2), :
                ]

    def send_even(l):
        for p in range(PIECES):
            piece = even.at[l, core, pl.ds(p * SIDE, SIDE)]
            remote(piece, piece, even_put.at[l], even_sem.at[l, p], x, partner).start()

    extract(layer_of(first_forward, 0))
    beside = (x > 0).astype(jnp.int32) + (x < sections - 1).astype(jnp.int32)
    pl.semaphore_wait(barrier, CHIPS + beside)

    mixed_copies = [
        remote(src, mixed.at[core, pl.ds(4 * j, 4)], mixed_put.at[j], mixed_sem.at[j], x, partner)
        for j, src in enumerate((forcing.at[:, theirs, :], cotangent.at[:, theirs, :], factor))
    ]
    for copy in mixed_copies:
        copy.start()

    send_even(layer_of(first_forward, 0))

    @pl.when(x > 0)
    def _():
        pl.semaphore_signal(
            next_ready, inc=1, device_id={"stream": x - 1, "cross": me}, device_id_type=MESH
        )

    @pl.when(x < sections - 1)
    def _():
        pl.semaphore_signal(
            last_ready, inc=1, device_id={"stream": x + 1, "cross": me}, device_id_type=MESH
        )

    def planar(j):
        wait(mixed.at[0, pl.ds(4 * j, 4)], mixed_sem.at[j])
        tall = jnp.concatenate(
            [mixed[h, 4 * j : 4 * j + 4].reshape(LAYERS * HALF, ROWS) for h in range(2)], axis=-1
        )
        return permuted(tall, planar_of[...]).reshape(LAYERS, HALF, WIDE)

    def rows_of(g):
        return slice(g * PART, (g + 1) * PART)

    def send_forward(step, g):
        slot = lax.rem(step, LAYERS)
        for k in range(CHIPS - 1, 0, -1):
            remote(
                got_f.at[step, g, 0], got_f.at[slot, g, k], f_put.at[step, g],
                f_sem.at[slot, g, k], x + step // LAYERS, chip_at(k, 1) * 2 + core,
            ).start()

    drive[0:LAYERS] = planar(0)

    @pl.when(x == 0)
    def _():
        for g in range(SETS):
            got_f[0, g, 0] = drive[0, rows_of(g)]
            send_forward(0, g)

    def prepare(l):
        @pl.loop(0, PIECES)
        def _(p):
            wait(even.at[l, core, pl.ds(p * SIDE, SIDE)], even_sem.at[l, p])
            for j in range(SIDE):
                q = p * SIDE + j
                high, low = split_two(jnp.concatenate([even[l, 0, q], even[l, 1, q]], axis=0))
                both = jnp.concatenate([high, low], axis=0)
                weights[l, q] = jnp.dot(both, planar_of[...], preferred_element_type=F32).astype(BF16)

    sink[...] = planar(1)

    @pl.when(x == sections - 1)
    def _():
        carry[...] = sink[LAYERS - 1]

    middle = jnp.logical_and(x > 0, x < sections - 1).astype(jnp.int32)

    prepare(layer_of(first_forward, 0))

    @pl.loop(1, LAYERS)
    def _(i):
        extract(layer_of(first_forward, i))
        send_even(layer_of(first_forward, i))

    factors[0:LAYERS] = planar(2)

    @pl.when(x > 0)
    def _():
        remote(drive.at[0], drive.at[LAYERS], side_put.at[0], side_sem.at[0], x - 1, me).start()
        remote(factors.at[0], factors.at[LAYERS], side_put.at[1], side_sem.at[1], x - 1, me).start()

    @pl.loop(1, 1 + (LAYERS - 1) * middle)
    def _(i):
        prepare(layer_of(first_forward, i))

    def prepare_next(phase, i, forward):
        @pl.when(jnp.logical_and(jnp.logical_and(phase == 0, middle == 0), i < LAYERS - 1))
        def _():
            prepare(layer_of(forward, i + 1))

    def put_out(kind, l, value, out):
        real = permuted(value, real_of[...])
        out_put[kind, l, 0] = real[:, :ROWS]
        out_put[kind, l, 1] = real[:, ROWS:]
        out[l, mine, :] = out_put[kind, l, core]
        remote(
            out_put.at[kind, l, 1 - core], out_got.at[kind, l], out_put_sem.at[kind, l],
            out_sem.at[kind, l], x, partner,
        ).start()

    def wait_side(phase, l):
        @pl.when(jnp.logical_and(jnp.logical_and(l == LAYERS - 1, x < sections - 1), phase == 0))
        def _():
            wait(drive.at[LAYERS], side_sem.at[0])
            wait(factors.at[LAYERS], side_sem.at[1])

    def forward_set(l, g):
        @pl.when(jnp.logical_and(l == 0, x > 0))
        def _():
            wait(got_f.at[0, g, 0], f_sem.at[0, g, 0])

        total = jnp.zeros((4 * PART, WIDE), F32)
        for group in GROUPS:
            for k in group:
                if k > 0:
                    wait(got_f.at[l, g, k], f_sem.at[l, g, k])
            for k in group:
                value = got_f[l, g, k]
                turned = jnp.concatenate([value[:, ROWS:], -value[:, :ROWS]], axis=1)
                left = jnp.concatenate(split_two(jnp.concatenate([value, turned], axis=0)), axis=0)
                total = total + lax.dot_general(
                    left, weights[l, chip_at(k, -1)], (((1,), (1,)), ((), ())), preferred_element_type=F32
                )
        total = total[: 2 * PART] + total[2 * PART :]
        total = total[:, :ROWS] + total[:, ROWS:]
        result = jnp.concatenate([total[:PART], total[PART:]], axis=1)

        @pl.when(jnp.logical_or(l < LAYERS - 1, x < sections - 1))
        def _():
            got_f[l + 1, g, 0] = drive[l + 1, rows_of(g)] + factors[l + 1, rows_of(g)] * result
            send_forward(l + 1, g)

            @pl.when(l == LAYERS - 1)
            def _():
                remote(
                    got_f.at[LAYERS, g, 0], got_f.at[0, g, 0], f_put_self.at[g], f_sem.at[0, g, 0],
                    x + 1, me,
                ).start()

        return result

    def forward_step(phase, i):
        l = i
        wait_side(phase, l)

        @pl.when(jnp.logical_and(l == LAYERS - 1, x < sections - 1))
        def _():
            pl.semaphore_wait(next_ready, 1)

        result = jnp.concatenate([forward_set(l, g) for g in range(SETS)], axis=0)
        put_out(0, l, result, response)
        prepare_next(phase, i, jnp.bool_(True))

    def summed(slot, g):
        total = got_b[slot, g, 0]
        for group in GROUPS[1:]:
            for k in group:
                wait(got_b.at[slot, g, k], b_sem.at[slot, g, k])
            for k in group:
                total = total + got_b[slot, g, k]
        return total

    def backward_set(l, g):
        @pl.when(jnp.logical_or(l < LAYERS - 1, x < sections - 1))
        def _():
            @pl.when(l == LAYERS - 1)
            def _():
                wait(got_b.at[LAYERS, g, 0], b_sem.at[LAYERS, g, 0])

            total = summed(l + 1, g)
            totals[l + 1, rows_of(g)] = total
            carry[rows_of(g)] = sink[l, rows_of(g)] + factors[l + 1, rows_of(g)] * total

        value = carry[rows_of(g)]
        column = jnp.concatenate(
            split_two(jnp.concatenate([value[:, :ROWS], value[:, ROWS:]], axis=0)), axis=0
        )
        left = jnp.concatenate([column, column], axis=1)
        leaves = jnp.logical_and(l == 0, x > 0).astype(jnp.int32)
        slot = l + LAYERS * leaves
        for group in PUSHES:
            for k in group:
                part = jnp.dot(left, weights[l, chip_at(k, 1)], preferred_element_type=F32)
                part = part[: 2 * PART] + part[2 * PART :]
                real, imag = part[:PART], part[PART:]
                put_b[l, g, k] = jnp.concatenate(
                    [real[:, :ROWS] - imag[:, ROWS:], real[:, ROWS:] + imag[:, :ROWS]], axis=1
                )
            for k in group:
                if k > 0:
                    remote(
                        put_b.at[l, g, k], got_b.at[slot, g, k], b_put.at[l, g], b_sem.at[slot, g, k],
                        x - leaves, chip_at(k, 1) * 2 + core,
                    ).start()

        @pl.when(leaves > 0)
        def _():
            remote(
                put_b.at[l, g, 0], got_b.at[LAYERS, g, 0], b_put_self.at[g], b_sem.at[LAYERS, g, 0],
                x - 1, me,
            ).start()

        @pl.when(leaves == 0)
        def _():
            got_b[l, g, 0] = put_b[l, g, 0]

    def backward_step(phase, i):
        l = LAYERS - 1 - i
        wait_side(phase, l)

        @pl.when(jnp.logical_and(l == 0, x > 0))
        def _():
            pl.semaphore_wait(last_ready, 1)

        for g in range(SETS):
            backward_set(l, g)

        @pl.when(l < LAYERS - 1)
        def _():
            put_out(1, l + 1, totals[l + 1], gradient)

        @pl.when(jnp.logical_and(l == LAYERS - 1, x < sections - 1))
        def _():
            remote(totals.at[LAYERS], back, back_put, back_sem, x + 1, me).start()

        prepare_next(phase, i, jnp.bool_(False))

    @pl.loop(0, 2)
    def _(phase):
        forward = (phase == 0) == first_forward

        @pl.when(forward)
        def _():
            @pl.loop(0, LAYERS)
            def _(i):
                forward_step(phase, i)

        @pl.when(jnp.logical_not(forward))
        def _():
            @pl.loop(0, LAYERS)
            def _(i):
                backward_step(phase, i)

    @pl.when(x == 0)
    def _():
        for g in range(SETS):
            back[rows_of(g)] = summed(0, g)

    @pl.when(x > 0)
    def _():
        wait(back, back_sem)

    put_out(1, 0, back[...], gradient)
    for j in range(3):
        wait(mixed.at[0, pl.ds(4 * j, 4)], mixed_put.at[j])

    @pl.loop(0, LAYERS)
    def _(l):
        wait(even.at[l, core], even_put.at[l])
        for g in range(SETS):
            wait(put_b.at[l, g, pl.ds(1, CHIPS - 1)], b_put.at[l, g])

    for g in range(SETS):
        sent = got_f.at[0, g, pl.ds(1, CHIPS - 1)]

        @pl.when(x == 0)
        def _():
            wait(sent, f_put.at[0, g])

        @pl.loop(1, LAYERS)
        def _(l):
            wait(sent, f_put.at[l, g])

        @pl.when(x < sections - 1)
        def _():
            wait(sent, f_put.at[LAYERS, g])
            wait(got_f.at[0, g, 0], f_put_self.at[g])

        @pl.when(x > 0)
        def _():
            wait(got_b.at[0, g, 0], b_put_self.at[g])

    @pl.when(x < sections - 1)
    def _():
        wait(back, back_put)

    @pl.when(x > 0)
    def _():
        wait(drive.at[0], side_put.at[0])
        wait(factors.at[0], side_put.at[1])

    for kind, out in enumerate((response, gradient)):
        @pl.loop(0, LAYERS)
        def _(l):
            wait(out_got.at[kind, l], out_sem.at[kind, l])
            out[l, theirs, :] = out_got[kind, l]
            wait(out_got.at[kind, l], out_put_sem.at[kind, l])


def finish(response_in, gradient_in, response, gradient):
    response[...] = response_in[...]
    gradient[...] = gradient_in[...]


def shards(forcing, cotangent, inverses, flags):
    vmem = pl.BlockSpec(memory_space=pltpu.VMEM)
    dma = pltpu.SemaphoreType.DMA
    block = (HALF, WIDE)
    results = tuple(
        pl.pallas_call(
            kernel,
            out_shape=[jax.ShapeDtypeStruct(forcing.shape, F32)] * 2,
            in_specs=[pl.BlockSpec(memory_space=pl.ANY)] * 4,
            out_specs=[vmem, vmem],
            scratch_shapes=[
                pltpu.VMEM((LAYERS, 2 * HALF, ROWS), F32),
                pltpu.VMEM((LAYERS, 2 * HALF, ROWS), F32),
                pltpu.VMEM((LAYERS, ROWS // 2), jnp.int32),
                dma((3,)),
                pltpu.VMEM((LAYERS, 2 * CHIPS, ROWS, ROWS), F32),
                pltpu.VMEM((LAYERS, 2, CHIPS, ROWS // 2, WIDE), F32),
                pltpu.VMEM((LAYERS, CHIPS, WIDE, WIDE), BF16),
                pltpu.VMEM((WIDE, WIDE), BF16),
                pltpu.VMEM((WIDE, WIDE), BF16),
                pltpu.VMEM((8, ROWS), F32),
                pltpu.VMEM((LAYERS, HALF, ROWS), F32),
                pltpu.VMEM((2, 12, HALF, ROWS), F32),
                pltpu.VMEM((LAYERS + 1, *block), F32),
                pltpu.VMEM((LAYERS, *block), F32),
                pltpu.VMEM((LAYERS + 1, *block), F32),
                pltpu.VMEM((LAYERS + 1, SETS, CHIPS, PART, WIDE), F32),
                pltpu.VMEM((LAYERS, SETS, CHIPS, PART, WIDE), F32),
                pltpu.VMEM((LAYERS + 1, SETS, CHIPS, PART, WIDE), F32),
                pltpu.VMEM(block, F32),
                pltpu.VMEM((LAYERS + 1, *block), F32),
                pltpu.VMEM(block, F32),
                pltpu.VMEM((2, LAYERS, 2, HALF, ROWS), F32),
                pltpu.VMEM((2, LAYERS, HALF, ROWS), F32),
                dma((LAYERS,)),
                dma((LAYERS,)),
                dma((LAYERS, PIECES)),
                dma((3,)),
                dma((3,)),
                dma((2,)),
                dma((2,)),
                pltpu.SemaphoreType.REGULAR,
                pltpu.SemaphoreType.REGULAR,
                dma((LAYERS + 1, SETS)),
                dma((SETS,)),
                dma((LAYERS, SETS, CHIPS)),
                dma((LAYERS, SETS)),
                dma((SETS,)),
                dma((LAYERS + 1, SETS, CHIPS)),
                dma,
                dma,
                dma((2, LAYERS)),
                dma((2, LAYERS)),
            ],
            compiler_params=pltpu.CompilerParams(
                collective_id=0, has_side_effects=True, vmem_limit_bytes=57 << 20
            ),
        )(forcing, cotangent, flags, inverses)
    )
    return tuple(
        pl.pallas_call(
            finish,
            out_shape=[jax.ShapeDtypeStruct(forcing.shape, F32)] * 2,
            in_specs=[vmem, vmem],
            out_specs=[vmem, vmem],
        )(*results)
    )


def solution(mesh):
    in_specs = (
        P("stream", None, "cross"),
        P("stream", None, "cross"),
        P("stream", "cross", None),
        P("stream", "cross"),
    )
    out_specs = (P("stream", None, "cross"), P("stream", None, "cross"))
    return jax.shard_map(shards, mesh=mesh, in_specs=in_specs, out_specs=out_specs, check_vma=False)
```

```python
import jax
import jax.numpy as jnp
from jax import lax
from jax.experimental import pallas as pl
from jax.experimental.pallas import tpu as pltpu
from jax.sharding import PartitionSpec as P

MESH = pl.DeviceIdType.MESH
SIDE = 4
CHIPS = SIDE * SIDE
HOPS = sorted(
    ((dz, dy) for dz in range(SIDE) for dy in range(SIDE)),
    key=lambda d: min(d[0], SIDE - d[0]) + min(d[1], SIDE - d[1]),
)
GROUPS = ((0,), (1, 2), (3, 4), (5, 6), (7, 8), (9, 10), (11, 12), (13, 14), (15,))
PUSHES = ((15, 14, 13, 12, 11, 4, 3, 2, 1), (10, 9, 8, 7, 6, 5, 0))
LAYERS = 4
PIECES = CHIPS // SIDE
HALF = 16
SETS = 2
PART = HALF // SETS
ROWS = 128
WIDE = 256
F32, BF16 = jnp.float32, jnp.bfloat16


def penalty(flag_cells):
    return jnp.where(flag_cells == 0, 0.98, jnp.where(flag_cells == 1, 0.05, 0.5)).astype(F32)


def split_two(value):
    high = value.astype(BF16)
    return high, (value - high.astype(F32)).astype(BF16)


def permuted(value, table):
    high = value.astype(BF16)
    rest = value - high.astype(F32)
    mid = rest.astype(BF16)
    low = (rest - mid.astype(F32)).astype(BF16)
    return sum(jnp.dot(part, table, preferred_element_type=F32) for part in (high, mid, low))


def kernel(
    forcing_in, cotangent_in, flags_in, inverses, response, gradient,
    forcing, cotangent, flags, in_sem,
    own, even, weights, planar_of, real_of, cells, factor, mixed,
    drive, sink, factors, got_f, put_b, got_b, carry, totals, back, out_put, out_got,
    load_sem, even_put, even_sem, mixed_put, mixed_sem, side_put, side_sem,
    next_ready, last_ready, f_put, f_put_self, f_sem, b_put, b_put_self, b_sem, back_put, back_sem, out_put_sem, out_sem,
):
    x = lax.axis_index("stream")
    me = lax.axis_index("cross")
    sections = lax.axis_size("stream")
    core = lax.rem(me, 2)
    chip = me // 2
    zc, yc = chip // SIDE, lax.rem(chip, SIDE)
    partner = me + 1 - 2 * core

    def chip_at(k, sign):
        dz, dy = HOPS[k]
        return lax.rem(zc + sign * dz + SIDE, SIDE) * SIDE + lax.rem(yc + sign * dy + SIDE, SIDE)

    def wait(ref, sem):
        pltpu.make_async_copy(ref, ref, sem).wait()

    def remote(src, dst, send_sem, recv_sem, section, device):
        return pltpu.make_async_remote_copy(
            src_ref=src, dst_ref=dst, send_sem=send_sem, recv_sem=recv_sem,
            device_id={"stream": section, "cross": device}, device_id_type=MESH,
        )

    barrier = pltpu.get_barrier_semaphore()

    def greet(section, device):
        pl.semaphore_signal(
            barrier, inc=1, device_id={"stream": section, "cross": device}, device_id_type=MESH
        )

    greet(x, partner)

    @pl.loop(1, CHIPS)
    def _(o):
        greet(x, lax.rem(chip + o, CHIPS) * 2 + core)

    @pl.when(x > 0)
    def _():
        greet(x - 1, me)

    @pl.when(x < sections - 1)
    def _():
        greet(x + 1, me)

    first_forward = x < sections // 2
    inputs = ((forcing_in, forcing), (cotangent_in, cotangent), (flags_in, flags))
    for j, (src, dst) in enumerate(inputs):
        pltpu.make_async_copy(src, dst, in_sem.at[j]).start()

    def layer_of(forward, i):
        f = forward.astype(jnp.int32)
        return f * i + (1 - f) * (LAYERS - 1 - i)

    @pl.loop(0, LAYERS)
    def _(i):
        l = layer_of(first_forward, i)
        for j in range(2 * CHIPS):
            pltpu.make_async_copy(
                inverses.at[l, :, pl.ds(j * ROWS, ROWS)], own.at[l, j], load_sem.at[l]
            ).start()

    r = lax.broadcasted_iota(jnp.int32, (WIDE, WIDE), 0)
    k = lax.broadcasted_iota(jnp.int32, (WIDE, WIDE), 1)
    planar_of[...] = (r == 2 * (k % ROWS) + k // ROWS).astype(F32).astype(BF16)
    real_of[...] = (k == 2 * (r % ROWS) + r // ROWS).astype(F32).astype(BF16)
    mine = pl.ds(pl.multiple_of(HALF * core, HALF), HALF)
    theirs = pl.ds(pl.multiple_of(HALF * (1 - core), HALF), HALF)
    for j, (src, dst) in enumerate(inputs):
        pltpu.make_async_copy(src, dst, in_sem.at[j]).wait()
    cells[...] = jnp.zeros_like(cells)
    cells[0:LAYERS, 0 : ROWS // 2] = penalty(flags[...])
    twice = r[:ROWS, :ROWS] == k[:ROWS, :ROWS] // 2
    doubled = permuted(cells[...], twice.astype(F32).astype(BF16))
    for l in range(LAYERS):
        factor[l] = jnp.broadcast_to(doubled[l : l + 1], (HALF, ROWS))
    mixed[core, 0:4] = forcing[:, mine, :]
    mixed[core, 4:8] = cotangent[:, mine, :]
    mixed[core, 8:12] = factor[...]

    def extract(l):
        wait(own.at[l], load_sem.at[l])
        for q in range(CHIPS):
            for h in range(2):
                even[l, core, q, :, h * ROWS : (h + 1) * ROWS] = own[
                    l, 2 * q + h, pl.ds(0, ROWS // 2, stride=2), :
                ]

    def send_even(l):
        for p in range(PIECES):
            piece = even.at[l, core, pl.ds(p * SIDE, SIDE)]
            remote(piece, piece, even_put.at[l], even_sem.at[l, p], x, partner).start()

    extract(layer_of(first_forward, 0))
    beside = (x > 0).astype(jnp.int32) + (x < sections - 1).astype(jnp.int32)
    pl.semaphore_wait(barrier, CHIPS + beside)

    mixed_copies = [
        remote(src, mixed.at[core, pl.ds(4 * j, 4)], mixed_put.at[j], mixed_sem.at[j], x, partner)
        for j, src in enumerate((forcing.at[:, theirs, :], cotangent.at[:, theirs, :], factor))
    ]
    for copy in mixed_copies:
        copy.start()

    send_even(layer_of(first_forward, 0))

    @pl.when(x > 0)
    def _():
        pl.semaphore_signal(
            next_ready, inc=1, device_id={"stream": x - 1, "cross": me}, device_id_type=MESH
        )

    @pl.when(x < sections - 1)
    def _():
        pl.semaphore_signal(
            last_ready, inc=1, device_id={"stream": x + 1, "cross": me}, device_id_type=MESH
        )

    def planar(j):
        wait(mixed.at[0, pl.ds(4 * j, 4)], mixed_sem.at[j])
        tall = jnp.concatenate(
            [mixed[h, 4 * j : 4 * j + 4].reshape(LAYERS * HALF, ROWS) for h in range(2)], axis=-1
        )
        return permuted(tall, planar_of[...]).reshape(LAYERS, HALF, WIDE)

    def rows_of(g):
        return slice(g * PART, (g + 1) * PART)

    def send_forward(step, g):
        slot = lax.rem(step, LAYERS)
        for k in range(CHIPS - 1, 0, -1):
            remote(
                got_f.at[step, g, 0], got_f.at[slot, g, k], f_put.at[step, g],
                f_sem.at[slot, g, k], x + step // LAYERS, chip_at(k, 1) * 2 + core,
            ).start()

    drive[0:LAYERS] = planar(0)

    @pl.when(x == 0)
    def _():
        for g in range(SETS):
            got_f[0, g, 0] = drive[0, rows_of(g)]
            send_forward(0, g)

    def prepare(l):
        @pl.loop(0, PIECES)
        def _(p):
            wait(even.at[l, core, pl.ds(p * SIDE, SIDE)], even_sem.at[l, p])
            for j in range(SIDE):
                q = p * SIDE + j
                high, low = split_two(jnp.concatenate([even[l, 0, q], even[l, 1, q]], axis=0))
                both = jnp.concatenate([high, low], axis=0)
                weights[l, q] = jnp.dot(both, planar_of[...], preferred_element_type=F32).astype(BF16)

    sink[...] = planar(1)

    @pl.when(x == sections - 1)
    def _():
        carry[...] = sink[LAYERS - 1]

    middle = jnp.logical_and(x > 0, x < sections - 1).astype(jnp.int32)

    prepare(layer_of(first_forward, 0))

    @pl.loop(1, LAYERS)
    def _(i):
        extract(layer_of(first_forward, i))
        send_even(layer_of(first_forward, i))

    factors[0:LAYERS] = planar(2)

    @pl.when(x > 0)
    def _():
        remote(drive.at[0], drive.at[LAYERS], side_put.at[0], side_sem.at[0], x - 1, me).start()
        remote(factors.at[0], factors.at[LAYERS], side_put.at[1], side_sem.at[1], x - 1, me).start()

    @pl.loop(1, 1 + (LAYERS - 1) * middle)
    def _(i):
        prepare(layer_of(first_forward, i))

    def prepare_next(phase, i, forward):
        @pl.when(jnp.logical_and(jnp.logical_and(phase == 0, middle == 0), i < LAYERS - 1))
        def _():
            prepare(layer_of(forward, i + 1))

    def put_out(kind, l, value, out):
        real = permuted(value, real_of[...])
        out_put[kind, l, 0] = real[:, :ROWS]
        out_put[kind, l, 1] = real[:, ROWS:]
        out[l, mine, :] = out_put[kind, l, core]
        remote(
            out_put.at[kind, l, 1 - core], out_got.at[kind, l], out_put_sem.at[kind, l],
            out_sem.at[kind, l], x, partner,
        ).start()

    def wait_side(phase, l):
        @pl.when(jnp.logical_and(jnp.logical_and(l == LAYERS - 1, x < sections - 1), phase == 0))
        def _():
            wait(drive.at[LAYERS], side_sem.at[0])
            wait(factors.at[LAYERS], side_sem.at[1])

    def forward_set(l, g):
        @pl.when(jnp.logical_and(l == 0, x > 0))
        def _():
            wait(got_f.at[0, g, 0], f_sem.at[0, g, 0])

        total = jnp.zeros((4 * PART, WIDE), F32)
        for group in GROUPS:
            for k in group:
                if k > 0:
                    wait(got_f.at[l, g, k], f_sem.at[l, g, k])
            for k in group:
                value = got_f[l, g, k]
                turned = jnp.concatenate([value[:, ROWS:], -value[:, :ROWS]], axis=1)
                left = jnp.concatenate(split_two(jnp.concatenate([value, turned], axis=0)), axis=0)
                total = total + lax.dot_general(
                    left, weights[l, chip_at(k, -1)], (((1,), (1,)), ((), ())), preferred_element_type=F32
                )
        total = total[: 2 * PART] + total[2 * PART :]
        total = total[:, :ROWS] + total[:, ROWS:]
        result = jnp.concatenate([total[:PART], total[PART:]], axis=1)

        @pl.when(jnp.logical_or(l < LAYERS - 1, x < sections - 1))
        def _():
            got_f[l + 1, g, 0] = drive[l + 1, rows_of(g)] + factors[l + 1, rows_of(g)] * result
            send_forward(l + 1, g)

            @pl.when(l == LAYERS - 1)
            def _():
                remote(
                    got_f.at[LAYERS, g, 0], got_f.at[0, g, 0], f_put_self.at[g], f_sem.at[0, g, 0],
                    x + 1, me,
                ).start()

        return result

    def forward_step(phase, i):
        l = i
        wait_side(phase, l)

        @pl.when(jnp.logical_and(l == LAYERS - 1, x < sections - 1))
        def _():
            pl.semaphore_wait(next_ready, 1)

        result = jnp.concatenate([forward_set(l, g) for g in range(SETS)], axis=0)
        put_out(0, l, result, response)
        prepare_next(phase, i, jnp.bool_(True))

    def summed(slot, g):
        total = got_b[slot, g, 0]
        for group in GROUPS[1:]:
            for k in group:
                wait(got_b.at[slot, g, k], b_sem.at[slot, g, k])
            for k in group:
                total = total + got_b[slot, g, k]
        return total

    def backward_set(l, g):
        @pl.when(jnp.logical_or(l < LAYERS - 1, x < sections - 1))
        def _():
            @pl.when(l == LAYERS - 1)
            def _():
                wait(got_b.at[LAYERS, g, 0], b_sem.at[LAYERS, g, 0])

            total = summed(l + 1, g)
            totals[l + 1, rows_of(g)] = total
            carry[rows_of(g)] = sink[l, rows_of(g)] + factors[l + 1, rows_of(g)] * total

        value = carry[rows_of(g)]
        column = jnp.concatenate(
            split_two(jnp.concatenate([value[:, :ROWS], value[:, ROWS:]], axis=0)), axis=0
        )
        left = jnp.concatenate([column, column], axis=1)
        leaves = jnp.logical_and(l == 0, x > 0).astype(jnp.int32)
        slot = l + LAYERS * leaves
        for group in PUSHES:
            for k in group:
                part = jnp.dot(left, weights[l, chip_at(k, 1)], preferred_element_type=F32)
                part = part[: 2 * PART] + part[2 * PART :]
                real, imag = part[:PART], part[PART:]
                put_b[l, g, k] = jnp.concatenate(
                    [real[:, :ROWS] - imag[:, ROWS:], real[:, ROWS:] + imag[:, :ROWS]], axis=1
                )
            for k in group:
                if k > 0:
                    remote(
                        put_b.at[l, g, k], got_b.at[slot, g, k], b_put.at[l, g], b_sem.at[slot, g, k],
                        x - leaves, chip_at(k, 1) * 2 + core,
                    ).start()

        @pl.when(leaves > 0)
        def _():
            remote(
                put_b.at[l, g, 0], got_b.at[LAYERS, g, 0], b_put_self.at[g], b_sem.at[LAYERS, g, 0],
                x - 1, me,
            ).start()

        @pl.when(leaves == 0)
        def _():
            got_b[l, g, 0] = put_b[l, g, 0]

    def backward_step(phase, i):
        l = LAYERS - 1 - i
        wait_side(phase, l)

        @pl.when(jnp.logical_and(l == 0, x > 0))
        def _():
            pl.semaphore_wait(last_ready, 1)

        for g in range(SETS):
            backward_set(l, g)

        @pl.when(l < LAYERS - 1)
        def _():
            put_out(1, l + 1, totals[l + 1], gradient)

        @pl.when(jnp.logical_and(l == LAYERS - 1, x < sections - 1))
        def _():
            remote(totals.at[LAYERS], back, back_put, back_sem, x + 1, me).start()

        prepare_next(phase, i, jnp.bool_(False))

    @pl.loop(0, 2)
    def _(phase):
        forward = (phase == 0) == first_forward

        @pl.when(forward)
        def _():
            @pl.loop(0, LAYERS)
            def _(i):
                forward_step(phase, i)

        @pl.when(jnp.logical_not(forward))
        def _():
            @pl.loop(0, LAYERS)
            def _(i):
                backward_step(phase, i)

    @pl.when(x == 0)
    def _():
        for g in range(SETS):
            back[rows_of(g)] = summed(0, g)

    @pl.when(x > 0)
    def _():
        wait(back, back_sem)

    put_out(1, 0, back[...], gradient)
    for j in range(3):
        wait(mixed.at[0, pl.ds(4 * j, 4)], mixed_put.at[j])

    @pl.loop(0, LAYERS)
    def _(l):
        wait(even.at[l, core], even_put.at[l])
        for g in range(SETS):
            wait(put_b.at[l, g, pl.ds(1, CHIPS - 1)], b_put.at[l, g])

    for g in range(SETS):
        sent = got_f.at[0, g, pl.ds(1, CHIPS - 1)]

        @pl.when(x == 0)
        def _():
            wait(sent, f_put.at[0, g])

        @pl.loop(1, LAYERS)
        def _(l):
            wait(sent, f_put.at[l, g])

        @pl.when(x < sections - 1)
        def _():
            wait(sent, f_put.at[LAYERS, g])
            wait(got_f.at[0, g, 0], f_put_self.at[g])

        @pl.when(x > 0)
        def _():
            wait(got_b.at[0, g, 0], b_put_self.at[g])

    @pl.when(x < sections - 1)
    def _():
        wait(back, back_put)

    @pl.when(x > 0)
    def _():
        wait(drive.at[0], side_put.at[0])
        wait(factors.at[0], side_put.at[1])

    for kind, out in enumerate((response, gradient)):
        @pl.loop(0, LAYERS)
        def _(l):
            wait(out_got.at[kind, l], out_sem.at[kind, l])
            out[l, theirs, :] = out_got[kind, l]
            wait(out_got.at[kind, l], out_put_sem.at[kind, l])


def finish(response_in, gradient_in, response, gradient):
    response[...] = response_in[...]
    gradient[...] = gradient_in[...]


def shards(forcing, cotangent, inverses, flags):
    vmem = pl.BlockSpec(memory_space=pltpu.VMEM)
    dma = pltpu.SemaphoreType.DMA
    block = (HALF, WIDE)
    results = tuple(
        pl.pallas_call(
            kernel,
            out_shape=[jax.ShapeDtypeStruct(forcing.shape, F32)] * 2,
            in_specs=[pl.BlockSpec(memory_space=pl.ANY)] * 4,
            out_specs=[vmem, vmem],
            scratch_shapes=[
                pltpu.VMEM((LAYERS, 2 * HALF, ROWS), F32),
                pltpu.VMEM((LAYERS, 2 * HALF, ROWS), F32),
                pltpu.VMEM((LAYERS, ROWS // 2), jnp.int32),
                dma((3,)),
                pltpu.VMEM((LAYERS, 2 * CHIPS, ROWS, ROWS), F32),
                pltpu.VMEM((LAYERS, 2, CHIPS, ROWS // 2, WIDE), F32),
                pltpu.VMEM((LAYERS, CHIPS, WIDE, WIDE), BF16),
                pltpu.VMEM((WIDE, WIDE), BF16),
                pltpu.VMEM((WIDE, WIDE), BF16),
                pltpu.VMEM((8, ROWS), F32),
                pltpu.VMEM((LAYERS, HALF, ROWS), F32),
                pltpu.VMEM((2, 12, HALF, ROWS), F32),
                pltpu.VMEM((LAYERS + 1, *block), F32),
                pltpu.VMEM((LAYERS, *block), F32),
                pltpu.VMEM((LAYERS + 1, *block), F32),
                pltpu.VMEM((LAYERS + 1, SETS, CHIPS, PART, WIDE), F32),
                pltpu.VMEM((LAYERS, SETS, CHIPS, PART, WIDE), F32),
                pltpu.VMEM((LAYERS + 1, SETS, CHIPS, PART, WIDE), F32),
                pltpu.VMEM(block, F32),
                pltpu.VMEM((LAYERS + 1, *block), F32),
                pltpu.VMEM(block, F32),
                pltpu.VMEM((2, LAYERS, 2, HALF, ROWS), F32),
                pltpu.VMEM((2, LAYERS, HALF, ROWS), F32),
                dma((LAYERS,)),
                dma((LAYERS,)),
                dma((LAYERS, PIECES)),
                dma((3,)),
                dma((3,)),
                dma((2,)),
                dma((2,)),
                pltpu.SemaphoreType.REGULAR,
                pltpu.SemaphoreType.REGULAR,
                dma((LAYERS + 1, SETS)),
                dma((SETS,)),
                dma((LAYERS, SETS, CHIPS)),
                dma((LAYERS, SETS)),
                dma((SETS,)),
                dma((LAYERS + 1, SETS, CHIPS)),
                dma,
                dma,
                dma((2, LAYERS)),
                dma((2, LAYERS)),
            ],
            compiler_params=pltpu.CompilerParams(
                collective_id=0, has_side_effects=True, vmem_limit_bytes=50 << 20
            ),
        )(*(pltpu.with_memory_space_constraint(a, pltpu.HBM) for a in (forcing, cotangent, flags, inverses)))
    )
    return tuple(
        pl.pallas_call(
            finish,
            out_shape=[jax.ShapeDtypeStruct(forcing.shape, F32)] * 2,
            in_specs=[vmem, vmem],
            out_specs=[vmem, vmem],
            compiler_params=pltpu.CompilerParams(vmem_limit_bytes=4 << 20),
        )(*results)
    )


def solution(mesh):
    in_specs = (
        P("stream", None, "cross"),
        P("stream", None, "cross"),
        P("stream", "cross", None),
        P("stream", "cross"),
    )
    out_specs = (P("stream", None, "cross"), P("stream", None, "cross"))
    return jax.shard_map(shards, mesh=mesh, in_specs=in_specs, out_specs=out_specs, check_vma=False)
```

```python
import jax
import jax.numpy as jnp
from jax import lax
from jax.experimental import pallas as pl
from jax.experimental.pallas import tpu as pltpu
from jax.sharding import PartitionSpec as P

MESH = pl.DeviceIdType.MESH
SIDE = 4
CHIPS = SIDE * SIDE
HOPS = sorted(
    ((dz, dy) for dz in range(SIDE) for dy in range(SIDE)),
    key=lambda d: min(d[0], SIDE - d[0]) + min(d[1], SIDE - d[1]),
)
GROUPS = ((0,), (1, 2), (3, 4), (5, 6), (7, 8), (9, 10), (11, 12), (13, 14), (15,))
PUSHES = ((15, 14, 13, 12, 11, 10, 9), (4, 3, 2, 1, 8, 7, 6, 5, 0))
LAYERS = 4
PIECES = CHIPS // SIDE
HALF = 16
SETS = 2
PART = HALF // SETS
ROWS = 128
WIDE = 256
F32, BF16 = jnp.float32, jnp.bfloat16


def penalty(flag_cells):
    return jnp.where(flag_cells == 0, 0.98, jnp.where(flag_cells == 1, 0.05, 0.5)).astype(F32)


def split_two(value):
    high = value.astype(BF16)
    return high, (value - high.astype(F32)).astype(BF16)


def permuted(value, table):
    high = value.astype(BF16)
    rest = value - high.astype(F32)
    mid = rest.astype(BF16)
    low = (rest - mid.astype(F32)).astype(BF16)
    return sum(jnp.dot(part, table, preferred_element_type=F32) for part in (high, mid, low))


def kernel(
    forcing_in, cotangent_in, flags_in, inverses, response, gradient,
    forcing, cotangent, flags, in_sem,
    own, even, weights, planar_of, real_of, cells, factor, mixed,
    drive, sink, factors, got_f, put_b, got_b, carry, totals, back, out_put, out_got,
    load_sem, even_put, even_sem, mixed_put, mixed_sem, side_put, side_sem,
    next_ready, last_ready, f_put, f_put_self, f_sem, b_put, b_put_self, b_sem, back_put, back_sem, out_put_sem, out_sem,
):
    x = lax.axis_index("stream")
    me = lax.axis_index("cross")
    sections = lax.axis_size("stream")
    core = lax.rem(me, 2)
    chip = me // 2
    zc, yc = chip // SIDE, lax.rem(chip, SIDE)
    partner = me + 1 - 2 * core

    def chip_at(k, sign):
        dz, dy = HOPS[k]
        return lax.rem(zc + sign * dz + SIDE, SIDE) * SIDE + lax.rem(yc + sign * dy + SIDE, SIDE)

    def wait(ref, sem):
        pltpu.make_async_copy(ref, ref, sem).wait()

    def remote(src, dst, send_sem, recv_sem, section, device):
        return pltpu.make_async_remote_copy(
            src_ref=src, dst_ref=dst, send_sem=send_sem, recv_sem=recv_sem,
            device_id={"stream": section, "cross": device}, device_id_type=MESH,
        )

    barrier = pltpu.get_barrier_semaphore()

    def greet(section, device):
        pl.semaphore_signal(
            barrier, inc=1, device_id={"stream": section, "cross": device}, device_id_type=MESH
        )

    greet(x, partner)

    @pl.loop(1, CHIPS)
    def _(o):
        greet(x, lax.rem(chip + o, CHIPS) * 2 + core)

    @pl.when(x > 0)
    def _():
        greet(x - 1, me)

    @pl.when(x < sections - 1)
    def _():
        greet(x + 1, me)

    first_forward = x < sections // 2
    inputs = ((forcing_in, forcing), (cotangent_in, cotangent), (flags_in, flags))
    for j, (src, dst) in enumerate(inputs):
        pltpu.make_async_copy(src, dst, in_sem.at[j]).start()

    def layer_of(forward, i):
        f = forward.astype(jnp.int32)
        return f * i + (1 - f) * (LAYERS - 1 - i)

    @pl.loop(0, LAYERS)
    def _(i):
        l = layer_of(first_forward, i)
        for j in range(2 * CHIPS):
            pltpu.make_async_copy(
                inverses.at[l, :, pl.ds(j * ROWS, ROWS)], own.at[l, j], load_sem.at[l]
            ).start()

    r = lax.broadcasted_iota(jnp.int32, (WIDE, WIDE), 0)
    k = lax.broadcasted_iota(jnp.int32, (WIDE, WIDE), 1)
    planar_of[...] = (r == 2 * (k % ROWS) + k // ROWS).astype(F32).astype(BF16)
    real_of[...] = (k == 2 * (r % ROWS) + r // ROWS).astype(F32).astype(BF16)
    mine = pl.ds(pl.multiple_of(HALF * core, HALF), HALF)
    theirs = pl.ds(pl.multiple_of(HALF * (1 - core), HALF), HALF)
    for j, (src, dst) in enumerate(inputs):
        pltpu.make_async_copy(src, dst, in_sem.at[j]).wait()
    cells[...] = jnp.zeros_like(cells)
    cells[0:LAYERS, 0 : ROWS // 2] = penalty(flags[...])
    twice = r[:ROWS, :ROWS] == k[:ROWS, :ROWS] // 2
    doubled = permuted(cells[...], twice.astype(F32).astype(BF16))
    for l in range(LAYERS):
        factor[l] = jnp.broadcast_to(doubled[l : l + 1], (HALF, ROWS))
    mixed[core, 0:4] = forcing[:, mine, :]
    mixed[core, 4:8] = cotangent[:, mine, :]
    mixed[core, 8:12] = factor[...]

    def extract(l):
        wait(own.at[l], load_sem.at[l])
        for q in range(CHIPS):
            for h in range(2):
                even[l, core, q, :, h * ROWS : (h + 1) * ROWS] = own[
                    l, 2 * q + h, pl.ds(0, ROWS // 2, stride=2), :
                ]

    def send_even(l):
        for p in range(PIECES):
            piece = even.at[l, core, pl.ds(p * SIDE, SIDE)]
            remote(piece, piece, even_put.at[l], even_sem.at[l, p], x, partner).start()

    extract(layer_of(first_forward, 0))
    beside = (x > 0).astype(jnp.int32) + (x < sections - 1).astype(jnp.int32)
    pl.semaphore_wait(barrier, CHIPS + beside)

    mixed_copies = [
        remote(src, mixed.at[core, pl.ds(4 * j, 4)], mixed_put.at[j], mixed_sem.at[j], x, partner)
        for j, src in enumerate((forcing.at[:, theirs, :], cotangent.at[:, theirs, :], factor))
    ]
    for copy in mixed_copies:
        copy.start()

    send_even(layer_of(first_forward, 0))

    @pl.when(x > 0)
    def _():
        pl.semaphore_signal(
            next_ready, inc=1, device_id={"stream": x - 1, "cross": me}, device_id_type=MESH
        )

    @pl.when(x < sections - 1)
    def _():
        pl.semaphore_signal(
            last_ready, inc=1, device_id={"stream": x + 1, "cross": me}, device_id_type=MESH
        )

    def planar(j):
        wait(mixed.at[0, pl.ds(4 * j, 4)], mixed_sem.at[j])
        tall = jnp.concatenate(
            [mixed[h, 4 * j : 4 * j + 4].reshape(LAYERS * HALF, ROWS) for h in range(2)], axis=-1
        )
        return permuted(tall, planar_of[...]).reshape(LAYERS, HALF, WIDE)

    def rows_of(g):
        return slice(g * PART, (g + 1) * PART)

    def send_forward(step, g):
        slot = lax.rem(step, LAYERS)
        for k in range(CHIPS - 1, 0, -1):
            remote(
                got_f.at[step, g, 0], got_f.at[slot, g, k], f_put.at[step, g],
                f_sem.at[slot, g, k], x + step // LAYERS, chip_at(k, 1) * 2 + core,
            ).start()

    drive[0:LAYERS] = planar(0)

    @pl.when(x == 0)
    def _():
        for g in range(SETS):
            got_f[0, g, 0] = drive[0, rows_of(g)]
            send_forward(0, g)

    def prepare(l):
        @pl.loop(0, PIECES)
        def _(p):
            wait(even.at[l, core, pl.ds(p * SIDE, SIDE)], even_sem.at[l, p])
            for j in range(SIDE):
                q = p * SIDE + j
                high, low = split_two(jnp.concatenate([even[l, 0, q], even[l, 1, q]], axis=0))
                both = jnp.concatenate([high, low], axis=0)
                weights[l, q] = jnp.dot(both, planar_of[...], preferred_element_type=F32).astype(BF16)

    sink[...] = planar(1)

    @pl.when(x == sections - 1)
    def _():
        carry[...] = sink[LAYERS - 1]

    middle = jnp.logical_and(x > 0, x < sections - 1).astype(jnp.int32)

    prepare(layer_of(first_forward, 0))

    @pl.loop(1, LAYERS)
    def _(i):
        extract(layer_of(first_forward, i))
        send_even(layer_of(first_forward, i))

    factors[0:LAYERS] = planar(2)

    @pl.when(x > 0)
    def _():
        remote(drive.at[0], drive.at[LAYERS], side_put.at[0], side_sem.at[0], x - 1, me).start()
        remote(factors.at[0], factors.at[LAYERS], side_put.at[1], side_sem.at[1], x - 1, me).start()

    @pl.loop(1, 1 + (LAYERS - 1) * middle)
    def _(i):
        prepare(layer_of(first_forward, i))

    def prepare_next(phase, i, forward):
        @pl.when(jnp.logical_and(jnp.logical_and(phase == 0, middle == 0), i < LAYERS - 1))
        def _():
            prepare(layer_of(forward, i + 1))

    def put_out(kind, l, value, out):
        real = permuted(value, real_of[...])
        out_put[kind, l, 0] = real[:, :ROWS]
        out_put[kind, l, 1] = real[:, ROWS:]
        out[l, mine, :] = out_put[kind, l, core]
        remote(
            out_put.at[kind, l, 1 - core], out_got.at[kind, l], out_put_sem.at[kind, l],
            out_sem.at[kind, l], x, partner,
        ).start()

    def wait_side(phase, l):
        @pl.when(jnp.logical_and(jnp.logical_and(l == LAYERS - 1, x < sections - 1), phase == 0))
        def _():
            wait(drive.at[LAYERS], side_sem.at[0])
            wait(factors.at[LAYERS], side_sem.at[1])

    def forward_set(l, g):
        @pl.when(jnp.logical_and(l == 0, x > 0))
        def _():
            wait(got_f.at[0, g, 0], f_sem.at[0, g, 0])

        total = jnp.zeros((4 * PART, WIDE), F32)
        for group in GROUPS:
            for k in group:
                if k > 0:
                    wait(got_f.at[l, g, k], f_sem.at[l, g, k])
            for k in group:
                value = got_f[l, g, k]
                turned = jnp.concatenate([value[:, ROWS:], -value[:, :ROWS]], axis=1)
                left = jnp.concatenate(split_two(jnp.concatenate([value, turned], axis=0)), axis=0)
                total = total + lax.dot_general(
                    left, weights[l, chip_at(k, -1)], (((1,), (1,)), ((), ())), preferred_element_type=F32
                )
        total = total[: 2 * PART] + total[2 * PART :]
        total = total[:, :ROWS] + total[:, ROWS:]
        result = jnp.concatenate([total[:PART], total[PART:]], axis=1)

        @pl.when(jnp.logical_or(l < LAYERS - 1, x < sections - 1))
        def _():
            got_f[l + 1, g, 0] = drive[l + 1, rows_of(g)] + factors[l + 1, rows_of(g)] * result
            send_forward(l + 1, g)

            @pl.when(l == LAYERS - 1)
            def _():
                remote(
                    got_f.at[LAYERS, g, 0], got_f.at[0, g, 0], f_put_self.at[g], f_sem.at[0, g, 0],
                    x + 1, me,
                ).start()

        return result

    def forward_step(phase, i):
        l = i
        wait_side(phase, l)

        @pl.when(jnp.logical_and(l == LAYERS - 1, x < sections - 1))
        def _():
            pl.semaphore_wait(next_ready, 1)

        result = jnp.concatenate([forward_set(l, g) for g in range(SETS)], axis=0)
        put_out(0, l, result, response)
        prepare_next(phase, i, jnp.bool_(True))

    def summed(slot, g):
        total = got_b[slot, g, 0]
        for group in GROUPS[1:]:
            for k in group:
                wait(got_b.at[slot, g, k], b_sem.at[slot, g, k])
            for k in group:
                total = total + got_b[slot, g, k]
        return total

    def backward_set(l, g):
        @pl.when(jnp.logical_or(l < LAYERS - 1, x < sections - 1))
        def _():
            @pl.when(l == LAYERS - 1)
            def _():
                wait(got_b.at[LAYERS, g, 0], b_sem.at[LAYERS, g, 0])

            total = summed(l + 1, g)
            totals[l + 1, rows_of(g)] = total
            carry[rows_of(g)] = sink[l, rows_of(g)] + factors[l + 1, rows_of(g)] * total

        value = carry[rows_of(g)]
        column = jnp.concatenate(
            split_two(jnp.concatenate([value[:, :ROWS], value[:, ROWS:]], axis=0)), axis=0
        )
        left = jnp.concatenate([column, column], axis=1)
        leaves = jnp.logical_and(l == 0, x > 0).astype(jnp.int32)
        slot = l + LAYERS * leaves
        for group in PUSHES:
            for k in group:
                part = jnp.dot(left, weights[l, chip_at(k, 1)], preferred_element_type=F32)
                part = part[: 2 * PART] + part[2 * PART :]
                real, imag = part[:PART], part[PART:]
                put_b[l, g, k] = jnp.concatenate(
                    [real[:, :ROWS] - imag[:, ROWS:], real[:, ROWS:] + imag[:, :ROWS]], axis=1
                )
            for k in group:
                if k > 0:
                    remote(
                        put_b.at[l, g, k], got_b.at[slot, g, k], b_put.at[l, g], b_sem.at[slot, g, k],
                        x - leaves, chip_at(k, 1) * 2 + core,
                    ).start()

        @pl.when(leaves > 0)
        def _():
            remote(
                put_b.at[l, g, 0], got_b.at[LAYERS, g, 0], b_put_self.at[g], b_sem.at[LAYERS, g, 0],
                x - 1, me,
            ).start()

        @pl.when(leaves == 0)
        def _():
            got_b[l, g, 0] = put_b[l, g, 0]

    def backward_step(phase, i):
        l = LAYERS - 1 - i
        wait_side(phase, l)

        @pl.when(jnp.logical_and(l == 0, x > 0))
        def _():
            pl.semaphore_wait(last_ready, 1)

        for g in range(SETS):
            backward_set(l, g)

        @pl.when(l < LAYERS - 1)
        def _():
            put_out(1, l + 1, totals[l + 1], gradient)

        @pl.when(jnp.logical_and(l == LAYERS - 1, x < sections - 1))
        def _():
            remote(totals.at[LAYERS], back, back_put, back_sem, x + 1, me).start()

        prepare_next(phase, i, jnp.bool_(False))

    @pl.loop(0, 2)
    def _(phase):
        forward = (phase == 0) == first_forward

        @pl.when(forward)
        def _():
            @pl.loop(0, LAYERS)
            def _(i):
                forward_step(phase, i)

        @pl.when(jnp.logical_not(forward))
        def _():
            @pl.loop(0, LAYERS)
            def _(i):
                backward_step(phase, i)

    @pl.when(x == 0)
    def _():
        for g in range(SETS):
            back[rows_of(g)] = summed(0, g)

    @pl.when(x > 0)
    def _():
        wait(back, back_sem)

    put_out(1, 0, back[...], gradient)
    for j in range(3):
        wait(mixed.at[0, pl.ds(4 * j, 4)], mixed_put.at[j])

    @pl.loop(0, LAYERS)
    def _(l):
        wait(even.at[l, core], even_put.at[l])
        for g in range(SETS):
            wait(put_b.at[l, g, pl.ds(1, CHIPS - 1)], b_put.at[l, g])

    for g in range(SETS):
        sent = got_f.at[0, g, pl.ds(1, CHIPS - 1)]

        @pl.when(x == 0)
        def _():
            wait(sent, f_put.at[0, g])

        @pl.loop(1, LAYERS)
        def _(l):
            wait(sent, f_put.at[l, g])

        @pl.when(x < sections - 1)
        def _():
            wait(sent, f_put.at[LAYERS, g])
            wait(got_f.at[0, g, 0], f_put_self.at[g])

        @pl.when(x > 0)
        def _():
            wait(got_b.at[0, g, 0], b_put_self.at[g])

    @pl.when(x < sections - 1)
    def _():
        wait(back, back_put)

    @pl.when(x > 0)
    def _():
        wait(drive.at[0], side_put.at[0])
        wait(factors.at[0], side_put.at[1])

    for kind, out in enumerate((response, gradient)):
        @pl.loop(0, LAYERS)
        def _(l):
            wait(out_got.at[kind, l], out_sem.at[kind, l])
            out[l, theirs, :] = out_got[kind, l]
            wait(out_got.at[kind, l], out_put_sem.at[kind, l])


def finish(response_in, gradient_in, response, gradient):
    response[...] = response_in[...]
    gradient[...] = gradient_in[...]


def shards(forcing, cotangent, inverses, flags):
    vmem = pl.BlockSpec(memory_space=pltpu.VMEM)
    dma = pltpu.SemaphoreType.DMA
    block = (HALF, WIDE)
    results = tuple(
        pl.pallas_call(
            kernel,
            out_shape=[jax.ShapeDtypeStruct(forcing.shape, F32)] * 2,
            in_specs=[pl.BlockSpec(memory_space=pl.ANY)] * 4,
            out_specs=[vmem, vmem],
            scratch_shapes=[
                pltpu.VMEM((LAYERS, 2 * HALF, ROWS), F32),
                pltpu.VMEM((LAYERS, 2 * HALF, ROWS), F32),
                pltpu.VMEM((LAYERS, ROWS // 2), jnp.int32),
                dma((3,)),
                pltpu.VMEM((LAYERS, 2 * CHIPS, ROWS, ROWS), F32),
                pltpu.VMEM((LAYERS, 2, CHIPS, ROWS // 2, WIDE), F32),
                pltpu.VMEM((LAYERS, CHIPS, WIDE, WIDE), BF16),
                pltpu.VMEM((WIDE, WIDE), BF16),
                pltpu.VMEM((WIDE, WIDE), BF16),
                pltpu.VMEM((8, ROWS), F32),
                pltpu.VMEM((LAYERS, HALF, ROWS), F32),
                pltpu.VMEM((2, 12, HALF, ROWS), F32),
                pltpu.VMEM((LAYERS + 1, *block), F32),
                pltpu.VMEM((LAYERS, *block), F32),
                pltpu.VMEM((LAYERS + 1, *block), F32),
                pltpu.VMEM((LAYERS + 1, SETS, CHIPS, PART, WIDE), F32),
                pltpu.VMEM((LAYERS, SETS, CHIPS, PART, WIDE), F32),
                pltpu.VMEM((LAYERS + 1, SETS, CHIPS, PART, WIDE), F32),
                pltpu.VMEM(block, F32),
                pltpu.VMEM((LAYERS + 1, *block), F32),
                pltpu.VMEM(block, F32),
                pltpu.VMEM((2, LAYERS, 2, HALF, ROWS), F32),
                pltpu.VMEM((2, LAYERS, HALF, ROWS), F32),
                dma((LAYERS,)),
                dma((LAYERS,)),
                dma((LAYERS, PIECES)),
                dma((3,)),
                dma((3,)),
                dma((2,)),
                dma((2,)),
                pltpu.SemaphoreType.REGULAR,
                pltpu.SemaphoreType.REGULAR,
                dma((LAYERS + 1, SETS)),
                dma((SETS,)),
                dma((LAYERS, SETS, CHIPS)),
                dma((LAYERS, SETS)),
                dma((SETS,)),
                dma((LAYERS + 1, SETS, CHIPS)),
                dma,
                dma,
                dma((2, LAYERS)),
                dma((2, LAYERS)),
            ],
            compiler_params=pltpu.CompilerParams(
                collective_id=0, has_side_effects=True, vmem_limit_bytes=50 << 20
            ),
        )(*(pltpu.with_memory_space_constraint(a, pltpu.HBM) for a in (forcing, cotangent, flags, inverses)))
    )
    return tuple(
        pl.pallas_call(
            finish,
            out_shape=[jax.ShapeDtypeStruct(forcing.shape, F32)] * 2,
            in_specs=[vmem, vmem],
            out_specs=[vmem, vmem],
            compiler_params=pltpu.CompilerParams(vmem_limit_bytes=4 << 20),
        )(*results)
    )


def solution(mesh):
    in_specs = (
        P("stream", None, "cross"),
        P("stream", None, "cross"),
        P("stream", "cross", None),
        P("stream", "cross"),
    )
    out_specs = (P("stream", None, "cross"), P("stream", None, "cross"))
    return jax.shard_map(shards, mesh=mesh, in_specs=in_specs, out_specs=out_specs, check_vma=False)
```
